512 devices in a mesh: blk: 64 (over y, z_lo, core), grp: 8 (over z_hi, x).
Axes of the slice: x: 4, y: 4, z: 16 (z_hi: 2, z_lo: 8; z = z_hi * 8 + z_lo), core: 2. Of those that a mesh axis runs over, the one named last changes fastest.
Arguments:
- occupied: bfloat16 [32768, 1024], P('blk'), may hold values from -6 to 6
- integrals: bfloat16 [64, 8, 3, 64, 4096], P('blk', 'grp'), may hold values from -0.75 to 0.75
- metric_inv: bfloat16 [65536, 1024], P('blk')
- pattern: int32 [64, 8, 3, 4], P('blk', 'grp'), may hold values from 0 to 63, as said below
- support: int32 [64, 8], P('blk'), may hold values from 0 to 1023, as said below
Outputs:
- exchange: float32 [32768, 512], P(('blk', 'grp'))
The draws below stay inside these ranges and needn't reach their ends.
Inputs may be any that keep to these rules, and one draw needn't show every extreme that they name: Field 0 of every slot of pattern[r, g] is a region within distance 3 of r along the closed chain of 64 regions; field 1 is below 8; field 2 is below 16; field 3 is 1 on a leading run of slots and 0 after it, and in every draw some basis block has all 3 slots live. `support`: the 8 orbitals of one region are distinct.
All inputs are finite; a program needn't handle non-finite values.
Results may differ from the reference program's by a relative error of at most 0.0045.
Values may be sent and summed in bfloat16 or wider, within the bound.
No kernel may reach another device: no remote copies, remote signals or barrier semaphores. Data moves between devices by JAX's collectives and lax.ppermute only.
A program may use at most 64 MiB of HBM per device.

```python
import math
import jax
import jax.numpy as jnp
from jax import lax

NOCC = 1024
BF = 64
AB = 64
AUXR = 1024
OSUP = 8
NT = 3
REACH = 3
REGIONS = 64
RB = 512
BASIS = 32768


def draw_metric_inv(key, part):
    key_diag, key_noise = jax.random.split(key)
    scale = 1.0 / math.sqrt(OSUP * AUXR)
    diagonal = jnp.exp(jax.random.uniform(key_diag, (REGIONS, AUXR), jnp.float32, 0.0, math.log(2.0)))
    noise_part = jax.random.normal(key_noise, (REGIONS, AUXR, AUXR), jnp.float32)
    mirrored = (noise_part + jnp.swapaxes(noise_part, 1, 2)) * (0.4 / math.sqrt(2.0 * AUXR))
    identity = (jnp.arange(AUXR)[:, None] == jnp.arange(AUXR)[None, :]).astype(jnp.float32)
    matrix = (diagonal[:, :, None] * identity[None] + mirrored) * scale
    return matrix.reshape(REGIONS * AUXR, AUXR).astype(jnp.bfloat16)


def draw_pattern(key, part):
    key_off, key_block, key_aux, key_live, key_full = jax.random.split(key, 5)
    groups = RB // BF
    shape = (REGIONS, groups, NT)
    region_ids = jnp.arange(REGIONS, dtype=jnp.int32)[:, None, None]
    offsets = jax.random.randint(key_off, shape, -REACH, REACH + 1, dtype=jnp.int32)
    source = (region_ids + offsets + REGIONS) % REGIONS
    basis_block = jax.random.randint(key_block, shape, 0, groups, dtype=jnp.int32)
    aux_block = jax.random.randint(key_aux, shape, 0, AUXR // AB, dtype=jnp.int32)
    live_count = jax.random.randint(key_live, (REGIONS, groups, 1), 1, NT + 1, dtype=jnp.int32)
    full_slot = jax.random.randint(key_full, (), 0, REGIONS * groups, dtype=jnp.int32)
    device_ids = jnp.arange(REGIONS * groups, dtype=jnp.int32).reshape(REGIONS, groups, 1)
    live_count = jnp.where(device_ids == full_slot, NT, live_count)
    live_flag = (jnp.arange(NT, dtype=jnp.int32)[None, None, :] < live_count).astype(jnp.int32)
    return jnp.stack([source, basis_block, aux_block, live_flag], axis=-1)


def draw_support(key, part):
    region_keys = jax.random.split(key, REGIONS)
    chosen = jax.vmap(lambda region_key: jax.random.permutation(region_key, NOCC)[:OSUP])(region_keys)
    chosen = chosen.astype(jnp.int32)
    picked_region = jax.random.randint(jax.random.fold_in(key, 7), (), 0, REGIONS, dtype=jnp.int32)
    region_ids = jnp.arange(REGIONS, dtype=jnp.int32)[:, None]
    highest = (chosen - chosen[:, :1] + NOCC - 1) % NOCC
    lowest = (chosen - chosen[:, :1] + NOCC) % NOCC
    result = jnp.where(region_ids == picked_region, highest, chosen)
    result = jnp.where(region_ids == (picked_region + 1) % REGIONS, lowest, result)
    return result


def levels(stream_key, dims, pieces, low, largest):
    level = 1.0
    for axis_at, parts in pieces:
        heights = jax.random.uniform(jax.random.fold_in(jax.random.fold_in(stream_key, 6), axis_at), (parts,), jnp.float32, low / len(pieces), largest / len(pieces))
        level = level * jnp.repeat(jnp.exp(heights), dims[axis_at] // parts).reshape((-1,) + (1,) * (len(dims) - 1 - axis_at))
    return level


def scatter_about(own_key, dims, scale, limit, cuts=(), kind=jnp.bfloat16):
    values = jax.random.normal(own_key, dims, jnp.float32) * scale
    if len(cuts) > 0:
        values = levels(own_key, dims, cuts, -0.22, 0.18) * values
    return jnp.clip(values, min=-limit, max=limit).astype(kind)


def setup_inputs(seed: int = 0) -> dict:
    key_list = jax.random.split(jax.random.key(seed), 6)
    occupied = scatter_about(key_list[0], (BASIS, NOCC), 1.0, 6.0, ((0, 64),))
    integrals = scatter_about(key_list[1], (REGIONS, RB // BF, NT, BF, BF * AB), 0.125, 0.75, ((0, 64), (1, 8)))
    metric_inv = draw_metric_inv(jax.random.fold_in(key_list[5], 71), 0)
    pattern = draw_pattern(jax.random.fold_in(key_list[5], 71), 0)
    support = draw_support(jax.random.fold_in(key_list[5], 71), 0)
    return {"occupied": occupied, "integrals": integrals, "metric_inv": metric_inv, "pattern": pattern, "support": support}


def reference(occupied, integrals, metric_inv, pattern, support):
    groups = RB // BF
    aux_blocks = AUXR // AB

    def region_rows(region):
        orbitals = support[region]
        tile_stack = integrals[region]
        slot_table = pattern[region]

        def tile_product(slot_fields, tile_data):
            first_row = (slot_fields[0] * RB + slot_fields[1] * BF).astype(jnp.int32)
            basis_rows = lax.dynamic_slice_in_dim(occupied, first_row, BF, 0)
            picked = jnp.take(basis_rows, orbitals, axis=1).astype(jnp.float32)
            return jnp.einsum("mi,mx->ix", picked, tile_data.astype(jnp.float32))

        def slot_weight(slot_fields):
            weight = (jnp.arange(aux_blocks, dtype=jnp.int32) == slot_fields[2]).astype(jnp.float32)
            return weight * slot_fields[3].astype(jnp.float32)

        products = jax.vmap(jax.vmap(tile_product))(slot_table, tile_stack)
        weights = jax.vmap(jax.vmap(slot_weight))(slot_table)
        summed = jnp.einsum("gta,gtix->gaix", weights, products)
        half_coef = summed.reshape(groups, aux_blocks, OSUP, BF, AB).transpose(0, 2, 3, 1, 4)
        half_coef = half_coef.reshape(groups, OSUP, BF, AUXR).astype(jnp.bfloat16)
        inverse = lax.dynamic_slice_in_dim(metric_inv, (region * AUXR).astype(jnp.int32), AUXR, 0)
        fitted = jnp.einsum("ginp,pq->ginq", half_coef.astype(jnp.float32), inverse.astype(jnp.float32))
        fitted = fitted.astype(jnp.bfloat16)
        exchange_block = jnp.einsum("ginq,himq->gnhm", half_coef.astype(jnp.float32), fitted.astype(jnp.float32))
        return exchange_block.reshape(RB, RB)

    blocks = lax.map(region_rows, jnp.arange(REGIONS, dtype=jnp.int32))
    return blocks.reshape(REGIONS * RB, RB)
```

```python
import jax
import jax.numpy as jnp
from jax import lax
from jax.experimental import pallas as pl
from jax.experimental.pallas import tpu as pltpu
from jax.sharding import PartitionSpec as P


BF = 64
AB = 64
AUXR = 1024
OSUP = 8
NT = 3
REACH = 3
XN = 4
DATA = OSUP * BF * NT * AB // 128
ROWS = DATA + 16
F32 = jnp.float32
BF16 = jnp.bfloat16


def near(region, group, offset, regions, zlo):
    target = region + offset
    step = target // 2 - region // 2
    z = (group // XN) * zlo + (region // 2) % zlo
    z = (z + step) % (2 * zlo)
    return (target % regions) * (2 * XN) + (z // zlo) * XN + group % XN


def offset_of(x, j):
    offset = x - REACH + XN * j
    return offset if offset <= REACH else 0


def request_pairs(j, regions):
    zlo = 8
    return [
        (r * 8 + g, near(r, g, offset_of(g % XN, j), regions, zlo))
        for r in range(regions)
        for g in range(2 * XN)
    ]


def contribution_kernel(region_ref, pattern_ref, window_ref, integrals_ref, out_ref, sa_ref, sb_ref):
    region = region_ref[0]
    a = [pattern_ref[0, 0, t, 2] for t in range(NT)]
    live = [pattern_ref[0, 0, t, 3] for t in range(NT)]
    lane8 = lax.broadcasted_iota(jnp.int32, (OSUP, 128), 1)
    low8 = lane8 < 64

    def tile(t, want_high):
        slot = (pattern_ref[0, 0, t, 0] - region + 64 + REACH) % 64
        m = pattern_ref[0, 0, t, 1]
        part = window_ref[
            slot % XN, slot // XN, :, pl.ds(pl.multiple_of((m // 2) * 128, 128), 128)
        ].astype(F32)
        return pltpu.roll(part, 64 * ((m % 2) ^ want_high), 1)

    chunk0 = jnp.where(low8, tile(0, 0), tile(1, 1))
    chunk1 = tile(2, 0)[:, :64]
    rep = [jnp.int32(0)]
    rep.append(jnp.where(a[1] == a[0], 0, 1))
    rep.append(jnp.where(a[2] == a[0], 0, jnp.where(a[2] == a[1], 1, 2)))
    rows = []
    for t in range(NT):
        w = [jnp.where(rep[u] == t, live[u], 0).astype(F32) for u in range(NT)]
        first = chunk0 * jnp.where(low8, w[0], w[1])
        rows.append(jnp.concatenate([first, chunk1 * w[2]], axis=1))
    lhs = jnp.concatenate(rows, axis=0).astype(BF16)
    tiles = integrals_ref[0, 0].reshape(NT * BF, BF * AB)
    c = jnp.dot(lhs, tiles, preferred_element_type=F32)
    for k in range(BF * AB // 128):
        v = [c[t * 8 : (t + 1) * 8, k * 128 : (k + 1) * 128] for t in range(NT)]
        s0, s1, s2 = [pltpu.roll(u, 64, 1) for u in v]
        half = pltpu.roll(v[2], 4, 0)
        half_s = pltpu.roll(s2, 4, 0)
        sa_ref[pl.ds(2 * k, OSUP, stride=BF), :] = jnp.where(low8, v[0], s1)
        sa_ref[pl.ds(2 * k + 1, OSUP, stride=BF), :] = jnp.where(low8, s0, v[1])
        sb_ref[pl.ds(2 * k, OSUP // 2, stride=BF), :] = jnp.where(low8, v[2], half_s)[: OSUP // 2]
        sb_ref[pl.ds(2 * k + 1, OSUP // 2, stride=BF), :] = jnp.where(low8, s2, half)[: OSUP // 2]
    out_ref[0:512, :] = sa_ref[...].astype(BF16)
    out_ref[512:768, :] = sb_ref[...].astype(BF16)
    lane = lax.broadcasted_iota(jnp.int32, (16, 128), 1)
    tag = jnp.where(lane == 0, a[0], jnp.where(lane == 1, a[1], a[2]))
    out_ref[768:784, :] = tag.astype(F32).astype(BF16)


def blocks_of(tag_row):
    row = tag_row.astype(F32)
    lane = lax.broadcasted_iota(jnp.int32, row.shape, 1)
    return [jnp.sum(jnp.where(lane == t, row, 0.0)).astype(jnp.int32) for t in range(NT)]


def weights_of(metric_ref, rows, cols):
    low = lax.broadcasted_iota(jnp.int32, (AB, 128), 1) < 64
    zero = jnp.zeros((AB, 128), F32)

    def piece(p, q, want_high):
        part = metric_ref[p, :, pl.ds(pl.multiple_of((q // 2) * 128, 128), 128)].astype(F32)
        return pltpu.roll(part, 64 * ((q % 2) ^ want_high), 1)

    lo, hi = [], []
    for p in rows:
        first = jnp.where(low, piece(p, cols[0], 0), piece(p, cols[1], 1))
        second = piece(p, cols[2], 0)
        lo.append(jnp.concatenate([first, jnp.where(low, second, zero)], axis=1))
        hi.append(jnp.concatenate([first, jnp.where(low, zero, pltpu.roll(second, 64, 1))], axis=1))
    blank = jnp.zeros((AB, 256), F32)
    lo = jnp.concatenate(lo + [blank], axis=0).astype(BF16)
    hi = jnp.concatenate(hi[:2] + [blank, hi[2]], axis=0).astype(BF16)
    return lo, hi


def halves(a_part, b_part):
    lo = jnp.concatenate([a_part[0:256], b_part], axis=1)
    hi = jnp.concatenate([a_part[256:512], b_part], axis=1)
    return lo, hi


def by_orbital(lo, hi):
    parts = [lo[i * 64 : (i + 1) * 64] for i in range(4)] + [hi[i * 64 : (i + 1) * 64] for i in range(4)]
    return jnp.concatenate(parts, axis=1)


def fitted_of(lo, hi, wlo, whi):
    flo = jnp.dot(lo, wlo, preferred_element_type=F32).astype(BF16)
    fhi = jnp.dot(hi, whi, preferred_element_type=F32).astype(BF16)
    return by_orbital(flo, fhi)


NT_DIMS = (((1,), (1,)), ((), ()))


def early_kernel(own_ref, all_ref, metric_ref, out_ref):
    cols = blocks_of(own_ref[768:784, :][0:1])
    own = by_orbital(*halves(own_ref[0:512, :], own_ref[512:768, :]))
    fitted = []
    for x in range(XN):
        rows = blocks_of(all_ref[x, 768:784, :][0:1])
        wlo, whi = weights_of(metric_ref, rows, cols)
        lo, hi = halves(all_ref[x, 0:512, :], all_ref[x, 512:768, :])
        fitted.append(fitted_of(lo, hi, wlo, whi))
    fitted = jnp.concatenate(fitted, axis=0)
    out_ref[...] = lax.dot_general(own, fitted, NT_DIMS, preferred_element_type=F32)


def late_kernel(far_ref, all_ref, metric_ref, out_ref):
    rows = blocks_of(far_ref[768:784, :][0:1])
    lo, hi = halves(far_ref[0:512, :], far_ref[512:768, :])
    for x in range(XN):
        cols = blocks_of(all_ref[x, 768:784, :][0:1])
        wlo, whi = weights_of(metric_ref, rows, cols)
        fitted = fitted_of(lo, hi, wlo, whi)
        mine = by_orbital(*halves(all_ref[x, 0:512, :], all_ref[x, 512:768, :]))
        block = lax.dot_general(mine, fitted, NT_DIMS, preferred_element_type=F32)
        out_ref[x] = jnp.concatenate([block[0:32], block[32:64]], axis=1)


def join_kernel(group_ref, early_ref, late_ref, out_ref):
    high = group_ref[0] >= XN
    late = jnp.concatenate(
        [
            jnp.concatenate([late_ref[x][:, 0:64] for x in range(XN)], axis=1),
            jnp.concatenate([late_ref[x][:, 64:128] for x in range(XN)], axis=1),
        ],
        axis=0,
    )
    early = early_ref[...]
    out_ref[:, 0:256] = jnp.where(high, late, early)
    out_ref[:, 256:512] = jnp.where(high, early, late)


def smem():
    return pl.BlockSpec(memory_space=pltpu.SMEM)


def vmem():
    return pl.BlockSpec(memory_space=pltpu.VMEM)


def per_device(occupied, integrals, metric_inv, pattern, support):
    regions = lax.axis_size("blk")
    axes = ("blk", "grp")
    groups = [list(range(XN)), list(range(XN, 2 * XN))]
    region = lax.axis_index("blk").astype(jnp.int32).reshape(1)
    group = lax.axis_index("grp").astype(jnp.int32).reshape(1)

    def spread(value):
        value = jnp.broadcast_to(value[None], (XN,) + value.shape)
        return lax.all_to_all(value, "grp", 0, 0, axis_index_groups=groups)

    pairs = [request_pairs(j, regions) for j in range(2)]
    asked = [lax.ppermute(support, axes, pairs[j]) for j in range(2)]
    asked = jnp.concatenate(asked, axis=1)[0]
    pick = (asked[:, None] == jnp.arange(occupied.shape[1], dtype=jnp.int32)[None, :]).astype(BF16)
    selected = lax.dot_general(pick, occupied, NT_DIMS, preferred_element_type=F32).astype(BF16)
    back = [[(d, s) for s, d in p] for p in pairs]
    got = [lax.ppermute(selected[j * OSUP : (j + 1) * OSUP], axes, back[j]) for j in range(2)]
    window = spread(jnp.stack(got, 0))

    message = pl.pallas_call(
        contribution_kernel,
        out_shape=jax.ShapeDtypeStruct((ROWS, 128), BF16),
        in_specs=[smem(), smem(), vmem(), vmem()],
        out_specs=vmem(),
        scratch_shapes=[pltpu.VMEM((512, 128), F32), pltpu.VMEM((256, 128), F32)],
        name="contribution",
    )(region, pattern, window, integrals)

    far = lax.ppermute(message, "grp", [(g, (g + XN) % (2 * XN)) for g in range(2 * XN)])
    everyone = spread(message)
    metric = metric_inv.reshape(AUXR // AB, AB, AUXR)
    early = pl.pallas_call(
        early_kernel,
        out_shape=jax.ShapeDtypeStruct((BF, XN * BF), F32),
        in_specs=[vmem(), vmem(), vmem()],
        out_specs=vmem(),
        name="early",
    )(message, everyone, metric)
    late = pl.pallas_call(
        late_kernel,
        out_shape=jax.ShapeDtypeStruct((XN, BF // 2, 2 * BF), F32),
        in_specs=[vmem(), vmem(), vmem()],
        out_specs=vmem(),
        name="late",
    )(far, everyone, metric)
    late = lax.all_to_all(late, "grp", 0, 0, axis_index_groups=groups)
    return pl.pallas_call(
        join_kernel,
        out_shape=jax.ShapeDtypeStruct((BF, 2 * XN * BF), F32),
        in_specs=[smem(), vmem(), vmem()],
        out_specs=vmem(),
        name="join",
    )(group, early, late)


def solution(mesh):
    placed = (
        P("blk", None),
        P("blk", "grp", None, None, None),
        P("blk", None),
        P("blk", "grp", None, None),
        P("blk", None),
    )
    return jax.shard_map(
        per_device, mesh=mesh, in_specs=placed, out_specs=P(("blk", "grp"), None), check_vma=False
    )
```

```python
import jax
import jax.numpy as jnp
from jax import lax
from jax.experimental import pallas as pl
from jax.experimental.pallas import tpu as pltpu
from jax.sharding import PartitionSpec as P


BF = 64
AB = 64
AUXR = 1024
OSUP = 8
NT = 3
REACH = 3
XN = 4
DATA = OSUP * BF * NT * AB // 128
ROWS = DATA + 16
F32 = jnp.float32
BF16 = jnp.bfloat16


def near(region, group, offset, regions, zlo):
    target = region + offset
    step = target // 2 - region // 2
    z = (group // XN) * zlo + (region // 2) % zlo
    z = (z + step) % (2 * zlo)
    return (target % regions) * (2 * XN) + (z // zlo) * XN + group % XN


def partner_offset(region, x, j):
    distance, phase = ((1, 0), (1, 1), (2, 0), (2, 1))[x] if j == 0 else ((3, 0), (3, 1), (0, 0), (0, 1))[x]
    place = (region // 2) if distance == 2 else region
    return distance if (place + phase) % 2 == 0 else -distance


def request_pairs(j, regions):
    zlo = 8
    return [
        (r * 8 + g, near(r, g, partner_offset(r, g % XN, j), regions, zlo))
        for r in range(regions)
        for g in range(2 * XN)
    ]


def contribution_kernel(region_ref, pattern_ref, window_ref, integrals_ref, out_ref, sa_ref, sb_ref):
    region = region_ref[0]
    a = [pattern_ref[0, 0, t, 2] for t in range(NT)]
    live = [pattern_ref[0, 0, t, 3] for t in range(NT)]
    lane8 = lax.broadcasted_iota(jnp.int32, (OSUP, 128), 1)
    low8 = lane8 < 64

    def tile(t, want_high):
        offset = (pattern_ref[0, 0, t, 0] - region + 64 + REACH) % 64 - REACH
        distance = jnp.abs(offset)
        place = jnp.where(distance == 2, region // 2, region)
        phase = jnp.where(offset > 0, place % 2, 1 - place % 2)
        x = jnp.where(distance == 2, 2, 0) + phase
        x = jnp.where(distance == 0, 2, x)
        j = jnp.where(distance == 1, 0, jnp.where(distance == 2, 0, 1))
        m = pattern_ref[0, 0, t, 1]
        part = window_ref[x, j, :, pl.ds(pl.multiple_of((m // 2) * 128, 128), 128)].astype(F32)
        return pltpu.roll(part, 64 * ((m % 2) ^ want_high), 1)

    chunk0 = jnp.where(low8, tile(0, 0), tile(1, 1))
    chunk1 = tile(2, 0)[:, :64]
    rep = [jnp.int32(0)]
    rep.append(jnp.where(a[1] == a[0], 0, 1))
    rep.append(jnp.where(a[2] == a[0], 0, jnp.where(a[2] == a[1], 1, 2)))
    rows = []
    for t in range(NT):
        w = [jnp.where(rep[u] == t, live[u], 0).astype(F32) for u in range(NT)]
        first = chunk0 * jnp.where(low8, w[0], w[1])
        rows.append(jnp.concatenate([first, chunk1 * w[2]], axis=1))
    lhs = jnp.concatenate(rows, axis=0).astype(BF16)
    tiles = integrals_ref[0, 0].reshape(NT * BF, BF * AB)
    c = jnp.dot(lhs, tiles, preferred_element_type=F32)
    for k in range(BF * AB // 128):
        v = [c[t * 8 : (t + 1) * 8, k * 128 : (k + 1) * 128] for t in range(NT)]
        s0, s1, s2 = [pltpu.roll(u, 64, 1) for u in v]
        half = pltpu.roll(v[2], 4, 0)
        half_s = pltpu.roll(s2, 4, 0)
        sa_ref[pl.ds(2 * k, OSUP, stride=BF), :] = jnp.where(low8, v[0], s1)
        sa_ref[pl.ds(2 * k + 1, OSUP, stride=BF), :] = jnp.where(low8, s0, v[1])
        sb_ref[pl.ds(2 * k, OSUP // 2, stride=BF), :] = jnp.where(low8, v[2], half_s)[: OSUP // 2]
        sb_ref[pl.ds(2 * k + 1, OSUP // 2, stride=BF), :] = jnp.where(low8, s2, half)[: OSUP // 2]
    out_ref[0:512, :] = sa_ref[...].astype(BF16)
    out_ref[512:768, :] = sb_ref[...].astype(BF16)
    lane = lax.broadcasted_iota(jnp.int32, (16, 128), 1)
    tag = jnp.where(lane == 0, a[0], jnp.where(lane == 1, a[1], a[2]))
    out_ref[768:784, :] = tag.astype(F32).astype(BF16)


def blocks_of(tag_row):
    row = tag_row.astype(F32)
    lane = lax.broadcasted_iota(jnp.int32, row.shape, 1)
    return [jnp.sum(jnp.where(lane == t, row, 0.0)).astype(jnp.int32) for t in range(NT)]


def weights_of(metric_ref, rows, cols):
    low = lax.broadcasted_iota(jnp.int32, (AB, 128), 1) < 64
    zero = jnp.zeros((AB, 128), F32)

    def piece(p, q, want_high):
        part = metric_ref[p, :, pl.ds(pl.multiple_of((q // 2) * 128, 128), 128)].astype(F32)
        return pltpu.roll(part, 64 * ((q % 2) ^ want_high), 1)

    lo, hi = [], []
    for p in rows:
        first = jnp.where(low, piece(p, cols[0], 0), piece(p, cols[1], 1))
        second = piece(p, cols[2], 0)
        lo.append(jnp.concatenate([first, jnp.where(low, second, zero)], axis=1))
        hi.append(jnp.concatenate([first, jnp.where(low, zero, pltpu.roll(second, 64, 1))], axis=1))
    blank = jnp.zeros((AB, 256), F32)
    lo = jnp.concatenate(lo + [blank], axis=0).astype(BF16)
    hi = jnp.concatenate(hi[:2] + [blank, hi[2]], axis=0).astype(BF16)
    return lo, hi


def halves(a_part, b_part):
    lo = jnp.concatenate([a_part[0:256], b_part], axis=1)
    hi = jnp.concatenate([a_part[256:512], b_part], axis=1)
    return lo, hi


def by_orbital(lo, hi):
    parts = [lo[i * 64 : (i + 1) * 64] for i in range(4)] + [hi[i * 64 : (i + 1) * 64] for i in range(4)]
    return jnp.concatenate(parts, axis=1)


def fitted_of(lo, hi, wlo, whi):
    flo = jnp.dot(lo, wlo, preferred_element_type=F32).astype(BF16)
    fhi = jnp.dot(hi, whi, preferred_element_type=F32).astype(BF16)
    return by_orbital(flo, fhi)


NT_DIMS = (((1,), (1,)), ((), ()))


def early_kernel(own_ref, all_ref, metric_ref, out_ref):
    cols = blocks_of(own_ref[768:784, :][0:1])
    own = by_orbital(*halves(own_ref[0:512, :], own_ref[512:768, :]))
    fitted = []
    for x in range(XN):
        rows = blocks_of(all_ref[x, 768:784, :][0:1])
        wlo, whi = weights_of(metric_ref, rows, cols)
        lo, hi = halves(all_ref[x, 0:512, :], all_ref[x, 512:768, :])
        fitted.append(fitted_of(lo, hi, wlo, whi))
    fitted = jnp.concatenate(fitted, axis=0)
    out_ref[...] = lax.dot_general(own, fitted, NT_DIMS, preferred_element_type=F32)


def late_kernel(far_ref, all_ref, metric_ref, out_ref):
    rows = blocks_of(far_ref[768:784, :][0:1])
    lo, hi = halves(far_ref[0:512, :], far_ref[512:768, :])
    for x in range(XN):
        cols = blocks_of(all_ref[x, 768:784, :][0:1])
        wlo, whi = weights_of(metric_ref, rows, cols)
        fitted = fitted_of(lo, hi, wlo, whi)
        mine = by_orbital(*halves(all_ref[x, 0:512, :], all_ref[x, 512:768, :]))
        block = lax.dot_general(mine, fitted, NT_DIMS, preferred_element_type=F32)
        out_ref[x] = jnp.concatenate([block[0:32], block[32:64]], axis=1)


def join_kernel(group_ref, early_ref, late_ref, out_ref):
    high = group_ref[0] >= XN
    late = jnp.concatenate(
        [
            jnp.concatenate([late_ref[x][:, 0:64] for x in range(XN)], axis=1),
            jnp.concatenate([late_ref[x][:, 64:128] for x in range(XN)], axis=1),
        ],
        axis=0,
    )
    early = early_ref[...]
    out_ref[:, 0:256] = jnp.where(high, late, early)
    out_ref[:, 256:512] = jnp.where(high, early, late)


def smem():
    return pl.BlockSpec(memory_space=pltpu.SMEM)


def vmem():
    return pl.BlockSpec(memory_space=pltpu.VMEM)


def in_vmem(value):
    return pltpu.with_memory_space_constraint(value, pltpu.VMEM)


def per_device(occupied, integrals, metric_inv, pattern, support):
    regions = lax.axis_size("blk")
    axes = ("blk", "grp")
    groups = [list(range(XN)), list(range(XN, 2 * XN))]
    region = lax.axis_index("blk").astype(jnp.int32).reshape(1)
    group = lax.axis_index("grp").astype(jnp.int32).reshape(1)

    def spread(value):
        value = jnp.broadcast_to(value[None], (XN,) + value.shape)
        return lax.all_to_all(value, "grp", 0, 0, axis_index_groups=groups)

    pairs = [request_pairs(j, regions) for j in range(2)]
    asked = [lax.ppermute(support, axes, pairs[j]) for j in range(2)]
    asked = jnp.concatenate(asked, axis=1)[0]
    pick = (asked[:, None] == jnp.arange(occupied.shape[1], dtype=jnp.int32)[None, :]).astype(BF16)
    selected = lax.dot_general(pick, occupied, NT_DIMS, preferred_element_type=F32).astype(BF16)
    back = [[(d, s) for s, d in p] for p in pairs]
    got = [lax.ppermute(selected[j * OSUP : (j + 1) * OSUP], axes, back[j]) for j in range(2)]
    window = spread(jnp.stack(got, 0))

    message = pl.pallas_call(
        contribution_kernel,
        out_shape=jax.ShapeDtypeStruct((ROWS, 128), BF16),
        in_specs=[smem(), smem(), vmem(), vmem()],
        out_specs=vmem(),
        scratch_shapes=[pltpu.VMEM((512, 128), F32), pltpu.VMEM((256, 128), F32)],
        name="contribution",
    )(region, pattern, in_vmem(window), integrals)

    far = lax.ppermute(message, "grp", [(g, (g + XN) % (2 * XN)) for g in range(2 * XN)])
    everyone = spread(message)
    metric = metric_inv.reshape(AUXR // AB, AB, AUXR)
    early = pl.pallas_call(
        early_kernel,
        out_shape=jax.ShapeDtypeStruct((BF, XN * BF), F32),
        in_specs=[vmem(), vmem(), vmem()],
        out_specs=vmem(),
        name="early",
    )(message, in_vmem(everyone), metric)
    late = pl.pallas_call(
        late_kernel,
        out_shape=jax.ShapeDtypeStruct((XN, BF // 2, 2 * BF), F32),
        in_specs=[vmem(), vmem(), vmem()],
        out_specs=vmem(),
        name="late",
    )(in_vmem(far), in_vmem(everyone), metric)
    late = lax.all_to_all(late, "grp", 0, 0, axis_index_groups=groups)
    return pl.pallas_call(
        join_kernel,
        out_shape=jax.ShapeDtypeStruct((BF, 2 * XN * BF), F32),
        in_specs=[smem(), vmem(), vmem()],
        out_specs=vmem(),
        name="join",
    )(group, early, in_vmem(late))


def solution(mesh):
    placed = (
        P("blk", None),
        P("blk", "grp", None, None, None),
        P("blk", None),
        P("blk", "grp", None, None),
        P("blk", None),
    )
    return jax.shard_map(
        per_device, mesh=mesh, in_specs=placed, out_specs=P(("blk", "grp"), None), check_vma=False
    )
```

```python
import jax
import jax.numpy as jnp
from jax import lax
from jax.experimental import pallas as pl
from jax.experimental.pallas import tpu as pltpu
from jax.sharding import PartitionSpec as P


BF = 64
AB = 64
AUXR = 1024
OSUP = 8
NT = 3
XN = 4
DATA = OSUP * BF * NT * AB // 128
ROWS = DATA + 16
F32 = jnp.float32
BF16 = jnp.bfloat16


def chip_offset(chip, x):
    distance, phase = ((1, 0), (1, 1), (2, 0), (2, 1))[x]
    return distance if (chip // distance + phase) % 2 == 0 else -distance


def chip_pairs(regions, zlo):
    chips = regions // 2
    pairs = []
    for region in range(regions):
        for group in range(2 * XN):
            chip, core = region // 2, region % 2
            offset = chip_offset(chip, group % XN)
            z = ((group // XN) * zlo + chip % zlo + offset) % (2 * zlo)
            target = ((chip + offset) % chips) * 2 + core
            pairs.append((region * 2 * XN + group, target * 2 * XN + (z // zlo) * XN + group % XN))
    return pairs


def contribution_kernel(region_ref, pattern_ref, window_ref, own_ref, integrals_ref, out_ref, sa_ref, sb_ref):
    region = region_ref[0]
    a = [pattern_ref[0, 0, t, 2] for t in range(NT)]
    live = [pattern_ref[0, 0, t, 3] for t in range(NT)]
    lane8 = lax.broadcasted_iota(jnp.int32, (OSUP, 128), 1)
    low8 = lane8 < 64

    def tile(t, want_high):
        source = pattern_ref[0, 0, t, 0]
        offset = (source // 2 - region // 2 + 32 + 2) % 32 - 2
        distance = jnp.abs(offset)
        phase = jnp.where(distance == 2, region // 4, region // 2) % 2
        phase = jnp.where(offset > 0, phase, 1 - phase)
        x = jnp.where(distance == 2, 2, 0) + phase
        other = (source % 2) ^ (region % 2)
        m = pattern_ref[0, 0, t, 1]
        lanes = pl.ds(pl.multiple_of((m // 2) * 128, 128), 128)
        away = window_ref[x, other, :, lanes].astype(F32)
        home = own_ref[other, :, lanes].astype(F32)
        part = jnp.where(offset == 0, home, away)
        return pltpu.roll(part, 64 * ((m % 2) ^ want_high), 1)

    chunk0 = jnp.where(low8, tile(0, 0), tile(1, 1))
    chunk1 = tile(2, 0)[:, :64]
    rep = [jnp.int32(0)]
    rep.append(jnp.where(a[1] == a[0], 0, 1))
    rep.append(jnp.where(a[2] == a[0], 0, jnp.where(a[2] == a[1], 1, 2)))
    rows = []
    for t in range(NT):
        w = [jnp.where(rep[u] == t, live[u], 0).astype(F32) for u in range(NT)]
        first = chunk0 * jnp.where(low8, w[0], w[1])
        rows.append(jnp.concatenate([first, chunk1 * w[2]], axis=1))
    lhs = jnp.concatenate(rows, axis=0).astype(BF16)
    tiles = integrals_ref[0, 0].reshape(NT * BF, BF * AB)
    c = jnp.dot(lhs, tiles, preferred_element_type=F32)
    for k in range(BF * AB // 128):
        v = [c[t * 8 : (t + 1) * 8, k * 128 : (k + 1) * 128] for t in range(NT)]
        s0, s1, s2 = [pltpu.roll(u, 64, 1) for u in v]
        half = pltpu.roll(v[2], 4, 0)
        half_s = pltpu.roll(s2, 4, 0)
        sa_ref[pl.ds(2 * k, OSUP, stride=BF), :] = jnp.where(low8, v[0], s1)
        sa_ref[pl.ds(2 * k + 1, OSUP, stride=BF), :] = jnp.where(low8, s0, v[1])
        sb_ref[pl.ds(2 * k, OSUP // 2, stride=BF), :] = jnp.where(low8, v[2], half_s)[: OSUP // 2]
        sb_ref[pl.ds(2 * k + 1, OSUP // 2, stride=BF), :] = jnp.where(low8, s2, half)[: OSUP // 2]
    out_ref[0:512, :] = sa_ref[...].astype(BF16)
    out_ref[512:768, :] = sb_ref[...].astype(BF16)
    lane = lax.broadcasted_iota(jnp.int32, (16, 128), 1)
    tag = jnp.where(lane == 0, a[0], jnp.where(lane == 1, a[1], a[2]))
    out_ref[768:784, :] = tag.astype(F32).astype(BF16)


def blocks_of(tag_row):
    row = tag_row.astype(F32)
    lane = lax.broadcasted_iota(jnp.int32, row.shape, 1)
    return [jnp.sum(jnp.where(lane == t, row, 0.0)).astype(jnp.int32) for t in range(NT)]


def weights_of(metric_ref, rows, cols):
    low = lax.broadcasted_iota(jnp.int32, (AB, 128), 1) < 64
    zero = jnp.zeros((AB, 128), F32)

    def piece(p, q, want_high):
        part = metric_ref[p, :, pl.ds(pl.multiple_of((q // 2) * 128, 128), 128)].astype(F32)
        return pltpu.roll(part, 64 * ((q % 2) ^ want_high), 1)

    lo, hi = [], []
    for p in rows:
        first = jnp.where(low, piece(p, cols[0], 0), piece(p, cols[1], 1))
        second = piece(p, cols[2], 0)
        lo.append(jnp.concatenate([first, jnp.where(low, second, zero)], axis=1))
        hi.append(jnp.concatenate([first, jnp.where(low, zero, pltpu.roll(second, 64, 1))], axis=1))
    blank = jnp.zeros((AB, 256), F32)
    lo = jnp.concatenate(lo + [blank], axis=0).astype(BF16)
    hi = jnp.concatenate(hi[:2] + [blank, hi[2]], axis=0).astype(BF16)
    return lo, hi


def halves(a_part, b_part):
    lo = jnp.concatenate([a_part[0:256], b_part], axis=1)
    hi = jnp.concatenate([a_part[256:512], b_part], axis=1)
    return lo, hi


def by_orbital(lo, hi):
    parts = [lo[i * 64 : (i + 1) * 64] for i in range(4)] + [hi[i * 64 : (i + 1) * 64] for i in range(4)]
    return jnp.concatenate(parts, axis=1)


def fitted_of(lo, hi, wlo, whi):
    flo = jnp.dot(lo, wlo, preferred_element_type=F32).astype(BF16)
    fhi = jnp.dot(hi, whi, preferred_element_type=F32).astype(BF16)
    return by_orbital(flo, fhi)


NT_DIMS = (((1,), (1,)), ((), ()))


def early_kernel(own_ref, all_ref, metric_ref, out_ref):
    cols = blocks_of(own_ref[768:784, :][0:1])
    own = by_orbital(*halves(own_ref[0:512, :], own_ref[512:768, :]))
    fitted = []
    for x in range(XN):
        rows = blocks_of(all_ref[x, 768:784, :][0:1])
        wlo, whi = weights_of(metric_ref, rows, cols)
        lo, hi = halves(all_ref[x, 0:512, :], all_ref[x, 512:768, :])
        fitted.append(fitted_of(lo, hi, wlo, whi))
    fitted = jnp.concatenate(fitted, axis=0)
    out_ref[...] = lax.dot_general(own, fitted, NT_DIMS, preferred_element_type=F32)


def late_kernel(far_ref, all_ref, metric_ref, out_ref):
    rows = blocks_of(far_ref[768:784, :][0:1])
    lo, hi = halves(far_ref[0:512, :], far_ref[512:768, :])
    for x in range(XN):
        cols = blocks_of(all_ref[x, 768:784, :][0:1])
        wlo, whi = weights_of(metric_ref, rows, cols)
        fitted = fitted_of(lo, hi, wlo, whi)
        mine = by_orbital(*halves(all_ref[x, 0:512, :], all_ref[x, 512:768, :]))
        block = lax.dot_general(mine, fitted, NT_DIMS, preferred_element_type=F32)
        out_ref[x] = jnp.concatenate([block[0:32], block[32:64]], axis=1)


def join_kernel(group_ref, early_ref, late_ref, out_ref):
    high = group_ref[0] >= XN
    late = jnp.concatenate(
        [
            jnp.concatenate([late_ref[x][:, 0:64] for x in range(XN)], axis=1),
            jnp.concatenate([late_ref[x][:, 64:128] for x in range(XN)], axis=1),
        ],
        axis=0,
    )
    early = early_ref[...]
    out_ref[:, 0:256] = jnp.where(high, late, early)
    out_ref[:, 256:512] = jnp.where(high, early, late)


def smem():
    return pl.BlockSpec(memory_space=pltpu.SMEM)


def vmem():
    return pl.BlockSpec(memory_space=pltpu.VMEM)


def in_vmem(value):
    return pltpu.with_memory_space_constraint(value, pltpu.VMEM)


def per_device(occupied, integrals, metric_inv, pattern, support):
    regions = lax.axis_size("blk")
    axes = ("blk", "grp")
    groups = [list(range(XN)), list(range(XN, 2 * XN))]
    region = lax.axis_index("blk").astype(jnp.int32).reshape(1)
    group = lax.axis_index("grp").astype(jnp.int32).reshape(1)

    def spread(value):
        value = jnp.broadcast_to(value[None], (XN,) + value.shape)
        return lax.all_to_all(value, "grp", 0, 0, axis_index_groups=groups)

    def pick(orbitals):
        wanted = orbitals[0][:, None] == jnp.arange(occupied.shape[1], dtype=jnp.int32)[None, :]
        out = lax.dot_general(wanted.astype(BF16), occupied, NT_DIMS, preferred_element_type=F32)
        return out.astype(BF16)

    sibling = [(r, r ^ 1) for r in range(regions)]
    partner = chip_pairs(regions, 8)
    both = jnp.concatenate([support, lax.ppermute(support, "blk", sibling)], axis=1)
    asked = lax.ppermute(both, axes, partner)
    mine = pick(both)
    answer = lax.ppermute(pick(asked), axes, partner)
    fromsib = lax.ppermute(
        jnp.concatenate([answer[OSUP:], mine[OSUP:]], axis=0), "blk", sibling
    )
    window = spread(jnp.stack([answer[:OSUP], fromsib[:OSUP]], 0))
    own = jnp.stack([mine[:OSUP], fromsib[OSUP:]], 0)

    message = pl.pallas_call(
        contribution_kernel,
        out_shape=jax.ShapeDtypeStruct((ROWS, 128), BF16),
        in_specs=[smem(), smem(), vmem(), vmem(), vmem()],
        out_specs=vmem(),
        scratch_shapes=[pltpu.VMEM((512, 128), F32), pltpu.VMEM((256, 128), F32)],
        name="contribution",
    )(region, pattern, in_vmem(window), in_vmem(own), in_vmem(integrals))

    far = lax.ppermute(message, "grp", [(g, (g + XN) % (2 * XN)) for g in range(2 * XN)])
    everyone = spread(message)
    metric = in_vmem(metric_inv.reshape(AUXR // AB, AB, AUXR))
    early = pl.pallas_call(
        early_kernel,
        out_shape=jax.ShapeDtypeStruct((BF, XN * BF), F32),
        in_specs=[vmem(), vmem(), vmem()],
        out_specs=vmem(),
        name="early",
    )(message, in_vmem(everyone), metric)
    late = pl.pallas_call(
        late_kernel,
        out_shape=jax.ShapeDtypeStruct((XN, BF // 2, 2 * BF), F32),
        in_specs=[vmem(), vmem(), vmem()],
        out_specs=vmem(),
        name="late",
    )(in_vmem(far), in_vmem(everyone), metric)
    late = lax.all_to_all(late, "grp", 0, 0, axis_index_groups=groups)
    return pl.pallas_call(
        join_kernel,
        out_shape=jax.ShapeDtypeStruct((BF, 2 * XN * BF), F32),
        in_specs=[smem(), vmem(), vmem()],
        out_specs=vmem(),
        name="join",
    )(group, early, in_vmem(late))


def solution(mesh):
    placed = (
        P("blk", None),
        P("blk", "grp", None, None, None),
        P("blk", None),
        P("blk", "grp", None, None),
        P("blk", None),
    )
    return jax.shard_map(
        per_device, mesh=mesh, in_specs=placed, out_specs=P(("blk", "grp"), None), check_vma=False
    )
```

```python
import jax
import jax.numpy as jnp
from jax import lax
from jax.experimental import pallas as pl
from jax.experimental.pallas import tpu as pltpu
from jax.sharding import PartitionSpec as P


BF = 64
AB = 64
AUXR = 1024
OSUP = 8
NT = 3
REACH = 3
XN = 4
DATA = OSUP * BF * NT * AB // 128
ROWS = DATA + 16
F32 = jnp.float32
BF16 = jnp.bfloat16


TASKS = (((3, 0), (3, 1), (2, 0), (2, 1)), ((1, 0), (0, 0), (1, 1), (0, 0)))


def swap_pairs(j, regions, zlo):
    pairs = []
    for region in range(regions):
        for group in range(2 * XN):
            distance, phase = TASKS[j][group % XN]
            place = (region // 2 if distance == 2 else region) + phase
            target = region + (distance if place % 2 == 0 else -distance)
            z = (group // XN) * zlo + (region // 2) % zlo + target // 2 - region // 2
            copy = (z % (2 * zlo)) // zlo * XN + group % XN
            pairs.append((region * 2 * XN + group, (target % regions) * 2 * XN + copy))
    return pairs


def contribution_kernel(region_ref, pattern_ref, window_ref, integrals_ref, out_ref, all_ref, sa_ref, sb_ref):
    region = region_ref[0]
    a = [pattern_ref[0, 0, t, 2] for t in range(NT)]
    live = [pattern_ref[0, 0, t, 3] for t in range(NT)]
    lane8 = lax.broadcasted_iota(jnp.int32, (OSUP, 128), 1)
    low8 = lane8 < 64

    def tile(t, want_high):
        source = pattern_ref[0, 0, t, 0]
        offset = (source - region + 64 + REACH) % 64 - REACH
        distance = jnp.abs(offset)
        place = jnp.where(distance == 2, region // 2, region) % 2
        phase = jnp.where(offset > 0, place, 1 - place)
        x = jnp.where(distance == 3, phase, jnp.where(distance == 0, 1, 2 * phase))
        x = jnp.where(distance == 2, 2 + phase, x)
        j = jnp.where(distance > 1, 0, 1)
        m = pattern_ref[0, 0, t, 1]
        lanes = pl.ds(pl.multiple_of((m // 2) * 128, 128), 128)
        part = window_ref[x, j, :, lanes].astype(F32)
        return pltpu.roll(part, 64 * ((m % 2) ^ want_high), 1)

    chunk0 = jnp.where(low8, tile(0, 0), tile(1, 1))
    chunk1 = tile(2, 0)[:, :64]
    rep = [jnp.int32(0)]
    rep.append(jnp.where(a[1] == a[0], 0, 1))
    rep.append(jnp.where(a[2] == a[0], 0, jnp.where(a[2] == a[1], 1, 2)))
    rows = []
    for t in range(NT):
        w = [jnp.where(rep[u] == t, live[u], 0).astype(F32) for u in range(NT)]
        first = chunk0 * jnp.where(low8, w[0], w[1])
        rows.append(jnp.concatenate([first, chunk1 * w[2]], axis=1))
    lhs = jnp.concatenate(rows, axis=0).astype(BF16)
    tiles = integrals_ref[0, 0].reshape(NT * BF, BF * AB)
    c = jnp.dot(lhs, tiles, preferred_element_type=F32)
    for k in range(BF * AB // 128):
        v = [c[t * 8 : (t + 1) * 8, k * 128 : (k + 1) * 128] for t in range(NT)]
        s0, s1, s2 = [pltpu.roll(u, 64, 1) for u in v]
        half = pltpu.roll(v[2], 4, 0)
        half_s = pltpu.roll(s2, 4, 0)
        sa_ref[pl.ds(2 * k, OSUP, stride=BF), :] = jnp.where(low8, v[0], s1)
        sa_ref[pl.ds(2 * k + 1, OSUP, stride=BF), :] = jnp.where(low8, s0, v[1])
        sb_ref[pl.ds(2 * k, OSUP // 2, stride=BF), :] = jnp.where(low8, v[2], half_s)[: OSUP // 2]
        sb_ref[pl.ds(2 * k + 1, OSUP // 2, stride=BF), :] = jnp.where(low8, s2, half)[: OSUP // 2]
    a_part = sa_ref[...].astype(BF16)
    b_part = sb_ref[...].astype(BF16)
    lane = lax.broadcasted_iota(jnp.int32, (16, 128), 1)
    tag = jnp.where(lane == 0, a[0], jnp.where(lane == 1, a[1], a[2])).astype(F32).astype(BF16)
    out_ref[0:512, :] = a_part
    out_ref[512:768, :] = b_part
    out_ref[768:784, :] = tag
    for copy in range(XN):
        all_ref[copy, 0:512, :] = a_part
        all_ref[copy, 512:768, :] = b_part
        all_ref[copy, 768:784, :] = tag


def stage_kernel(*refs):
    half = len(refs) // 3
    copies = [
        pltpu.make_async_copy(refs[k], refs[half + k], refs[2 * half + k]) for k in range(half)
    ]
    for copy in copies:
        copy.start()
    for copy in copies:
        copy.wait()


def blocks_of(tag_row):
    row = tag_row.astype(F32)
    lane = lax.broadcasted_iota(jnp.int32, row.shape, 1)
    return [jnp.sum(jnp.where(lane == t, row, 0.0)).astype(jnp.int32) for t in range(NT)]


def weights_of(metric_ref, rows, cols):
    low = lax.broadcasted_iota(jnp.int32, (AB, 128), 1) < 64
    zero = jnp.zeros((AB, 128), F32)

    def piece(p, q, want_high):
        part = metric_ref[p, :, pl.ds(pl.multiple_of((q // 2) * 128, 128), 128)].astype(F32)
        return pltpu.roll(part, 64 * ((q % 2) ^ want_high), 1)

    lo, hi = [], []
    for p in rows:
        first = jnp.where(low, piece(p, cols[0], 0), piece(p, cols[1], 1))
        second = piece(p, cols[2], 0)
        lo.append(jnp.concatenate([first, jnp.where(low, second, zero)], axis=1))
        hi.append(jnp.concatenate([first, jnp.where(low, zero, pltpu.roll(second, 64, 1))], axis=1))
    blank = jnp.zeros((AB, 256), F32)
    lo = jnp.concatenate(lo + [blank], axis=0).astype(BF16)
    hi = jnp.concatenate(hi[:2] + [blank, hi[2]], axis=0).astype(BF16)
    return lo, hi


def halves(a_part, b_part):
    lo = jnp.concatenate([a_part[0:256], b_part], axis=1)
    hi = jnp.concatenate([a_part[256:512], b_part], axis=1)
    return lo, hi


def by_orbital(lo, hi):
    parts = [lo[i * 64 : (i + 1) * 64] for i in range(4)] + [hi[i * 64 : (i + 1) * 64] for i in range(4)]
    return jnp.concatenate(parts, axis=1)


def fitted_of(lo, hi, wlo, whi):
    flo = jnp.dot(lo, wlo, preferred_element_type=F32).astype(BF16)
    fhi = jnp.dot(hi, whi, preferred_element_type=F32).astype(BF16)
    return by_orbital(flo, fhi)


NT_DIMS = (((1,), (1,)), ((), ()))


def early_kernel(own_ref, all_ref, metric_ref, out_ref):
    cols = blocks_of(own_ref[768:784, :][0:1])
    own = by_orbital(*halves(own_ref[0:512, :], own_ref[512:768, :]))
    fitted = []
    for x in range(XN):
        rows = blocks_of(all_ref[x, 768:784, :][0:1])
        wlo, whi = weights_of(metric_ref, rows, cols)
        lo, hi = halves(all_ref[x, 0:512, :], all_ref[x, 512:768, :])
        fitted.append(fitted_of(lo, hi, wlo, whi))
    fitted = jnp.concatenate(fitted, axis=0)
    out_ref[...] = lax.dot_general(own, fitted, NT_DIMS, preferred_element_type=F32)


def late_kernel(far_ref, all_ref, metric_ref, out_ref):
    rows = blocks_of(far_ref[768:784, :][0:1])
    lo, hi = halves(far_ref[0:512, :], far_ref[512:768, :])
    for x in range(XN):
        cols = blocks_of(all_ref[x, 768:784, :][0:1])
        wlo, whi = weights_of(metric_ref, rows, cols)
        fitted = fitted_of(lo, hi, wlo, whi)
        mine = by_orbital(*halves(all_ref[x, 0:512, :], all_ref[x, 512:768, :]))
        block = lax.dot_general(mine, fitted, NT_DIMS, preferred_element_type=F32)
        out_ref[x] = jnp.concatenate([block[0:32], block[32:64]], axis=1)


def join_kernel(group_ref, early_ref, late_ref, out_ref):
    high = group_ref[0] >= XN
    late = jnp.concatenate(
        [
            jnp.concatenate([late_ref[x][:, 0:64] for x in range(XN)], axis=1),
            jnp.concatenate([late_ref[x][:, 64:128] for x in range(XN)], axis=1),
        ],
        axis=0,
    )
    early = early_ref[...]
    out_ref[:, 0:256] = jnp.where(high, late, early)
    out_ref[:, 256:512] = jnp.where(high, early, late)


def smem():
    return pl.BlockSpec(memory_space=pltpu.SMEM)


def vmem():
    return pl.BlockSpec(memory_space=pltpu.VMEM)


def in_vmem(value):
    return pltpu.with_memory_space_constraint(value, pltpu.VMEM)


def staged(parts):
    return pl.pallas_call(
        stage_kernel,
        out_shape=[pltpu.VMEM(p.shape, p.dtype) for p in parts],
        in_specs=[pl.BlockSpec(memory_space=pltpu.HBM)] * len(parts),
        out_specs=[vmem()] * len(parts),
        scratch_shapes=[pltpu.SemaphoreType.DMA] * len(parts),
        compiler_params=pltpu.CompilerParams(vmem_limit_bytes=16 * 2**20),
    )(*[pltpu.with_memory_space_constraint(p, pltpu.HBM) for p in parts])


def per_device(occupied, integrals, metric_inv, pattern, support):
    regions = lax.axis_size("blk")
    axes = ("blk", "grp")
    groups = [list(range(XN)), list(range(XN, 2 * XN))]
    region = lax.axis_index("blk").astype(jnp.int32).reshape(1)
    group = lax.axis_index("grp").astype(jnp.int32).reshape(1)

    def spread(value):
        value = jnp.broadcast_to(value[None], (XN,) + value.shape)
        return lax.all_to_all(value, "grp", 0, 0, axis_index_groups=groups)

    pairs = [swap_pairs(j, regions, 8) for j in range(2)]
    asked = []
    for j in range(2):
        asked.append(lax.ppermute(support, axes, pairs[j]))
    occupied, integrals = staged([occupied, integrals])
    asked = jnp.concatenate(asked, axis=1)[0]
    wanted = asked[:, None] == jnp.arange(occupied.shape[1], dtype=jnp.int32)[None, :]
    answer = lax.dot_general(wanted.astype(BF16), occupied, NT_DIMS, preferred_element_type=F32)
    answer = answer.astype(BF16)
    answer = [lax.ppermute(answer[j * OSUP : (j + 1) * OSUP], axes, pairs[j]) for j in range(2)]
    window = spread(jnp.stack(answer, 0))
    (metric,) = staged([metric_inv])
    metric = in_vmem(metric.reshape(AUXR // AB, AB, AUXR))

    message, copies = pl.pallas_call(
        contribution_kernel,
        out_shape=[
            pltpu.VMEM((ROWS, 128), BF16),
            jax.ShapeDtypeStruct((XN, ROWS, 128), BF16),
        ],
        in_specs=[smem(), smem(), vmem(), vmem()],
        out_specs=[vmem(), vmem()],
        scratch_shapes=[pltpu.VMEM((512, 128), F32), pltpu.VMEM((256, 128), F32)],
        name="contribution",
            compiler_params=pltpu.CompilerParams(vmem_limit_bytes=16 * 2**20),
    )(region, pattern, in_vmem(window), in_vmem(integrals))

    far = lax.ppermute(message, "grp", [(g, (g + XN) % (2 * XN)) for g in range(2 * XN)])
    everyone = lax.all_to_all(copies, "grp", 0, 0, axis_index_groups=groups)
    early = pl.pallas_call(
        early_kernel,
        out_shape=jax.ShapeDtypeStruct((BF, XN * BF), F32),
        in_specs=[vmem(), vmem(), vmem()],
        out_specs=vmem(),
        name="early",
        compiler_params=pltpu.CompilerParams(vmem_limit_bytes=16 * 2**20),
    )(in_vmem(message), in_vmem(everyone), metric)
    late = pl.pallas_call(
        late_kernel,
        out_shape=jax.ShapeDtypeStruct((XN, BF // 2, 2 * BF), F32),
        in_specs=[vmem(), vmem(), vmem()],
        out_specs=vmem(),
        name="late",
            compiler_params=pltpu.CompilerParams(vmem_limit_bytes=16 * 2**20),
    )(in_vmem(far), in_vmem(everyone), metric)
    late = lax.all_to_all(late, "grp", 0, 0, axis_index_groups=groups)
    return pl.pallas_call(
        join_kernel,
        out_shape=jax.ShapeDtypeStruct((BF, 2 * XN * BF), F32),
        in_specs=[smem(), vmem(), vmem()],
        out_specs=vmem(),
        name="join",
            compiler_params=pltpu.CompilerParams(vmem_limit_bytes=16 * 2**20),
    )(group, early, in_vmem(late))


def solution(mesh):
    placed = (
        P("blk", None),
        P("blk", "grp", None, None, None),
        P("blk", None),
        P("blk", "grp", None, None),
        P("blk", None),
    )
    return jax.shard_map(
        per_device, mesh=mesh, in_specs=placed, out_specs=P(("blk", "grp"), None), check_vma=False
    )
```

```python
import jax
import jax.numpy as jnp
from jax import lax
from jax.experimental import pallas as pl
from jax.experimental.pallas import tpu as pltpu
from jax.sharding import PartitionSpec as P


BF = 64
AB = 64
AUXR = 1024
OSUP = 8
NT = 3
REACH = 3
XN = 4
DATA = OSUP * BF * NT * AB // 128
ROWS = DATA + 16
F32 = jnp.float32
BF16 = jnp.bfloat16


TASKS = (((3, 0), (3, 1), (1, 1), (2, 1)), ((1, 0), (0, 0), (2, 0), (0, 0)))


def swap_pairs(j, regions, zlo):
    pairs = []
    for region in range(regions):
        for group in range(2 * XN):
            distance, phase = TASKS[j][group % XN]
            place = (region // 2 if distance == 2 else region) + phase
            target = region + (distance if place % 2 == 0 else -distance)
            z = (group // XN) * zlo + (region // 2) % zlo + target // 2 - region // 2
            copy = (z % (2 * zlo)) // zlo * XN + group % XN
            pairs.append((region * 2 * XN + group, (target % regions) * 2 * XN + copy))
    return pairs


def contribution_kernel(region_ref, pattern_ref, window_ref, integrals_ref, out_ref, all_ref, sa_ref, sb_ref):
    region = region_ref[0]
    a = [pattern_ref[0, 0, t, 2] for t in range(NT)]
    live = [pattern_ref[0, 0, t, 3] for t in range(NT)]
    lane8 = lax.broadcasted_iota(jnp.int32, (OSUP, 128), 1)
    low8 = lane8 < 64

    def tile(t, want_high):
        source = pattern_ref[0, 0, t, 0]
        offset = (source - region + 64 + REACH) % 64 - REACH
        distance = jnp.abs(offset)
        place = jnp.where(distance == 2, region // 2, region) % 2
        phase = jnp.where(offset > 0, place, 1 - place)
        x = jnp.where(distance == 3, phase, jnp.where(distance == 0, 1, 2 * phase))
        x = jnp.where(distance == 2, 2 + phase, x)
        first = jnp.where(distance == 1, phase, jnp.where(distance == 2, phase, distance // 3))
        j = 1 - first
        m = pattern_ref[0, 0, t, 1]
        lanes = pl.ds(pl.multiple_of((m // 2) * 128, 128), 128)
        part = window_ref[x, j, :, lanes].astype(F32)
        return pltpu.roll(part, 64 * ((m % 2) ^ want_high), 1)

    chunk0 = jnp.where(low8, tile(0, 0), tile(1, 1))
    chunk1 = tile(2, 0)[:, :64]
    rep = [jnp.int32(0)]
    rep.append(jnp.where(a[1] == a[0], 0, 1))
    rep.append(jnp.where(a[2] == a[0], 0, jnp.where(a[2] == a[1], 1, 2)))
    rows = []
    for t in range(NT):
        w = [jnp.where(rep[u] == t, live[u], 0).astype(F32) for u in range(NT)]
        first = chunk0 * jnp.where(low8, w[0], w[1])
        rows.append(jnp.concatenate([first, chunk1 * w[2]], axis=1))
    lhs = jnp.concatenate(rows, axis=0).astype(BF16)
    tiles = integrals_ref[0, 0].reshape(NT * BF, BF * AB)
    c = jnp.dot(lhs, tiles, preferred_element_type=F32)
    for k in range(BF * AB // 128):
        v = [c[t * 8 : (t + 1) * 8, k * 128 : (k + 1) * 128] for t in range(NT)]
        s0, s1, s2 = [pltpu.roll(u, 64, 1) for u in v]
        half = pltpu.roll(v[2], 4, 0)
        half_s = pltpu.roll(s2, 4, 0)
        sa_ref[pl.ds(2 * k, OSUP, stride=BF), :] = jnp.where(low8, v[0], s1)
        sa_ref[pl.ds(2 * k + 1, OSUP, stride=BF), :] = jnp.where(low8, s0, v[1])
        sb_ref[pl.ds(2 * k, OSUP // 2, stride=BF), :] = jnp.where(low8, v[2], half_s)[: OSUP // 2]
        sb_ref[pl.ds(2 * k + 1, OSUP // 2, stride=BF), :] = jnp.where(low8, s2, half)[: OSUP // 2]
    a_part = sa_ref[...].astype(BF16)
    b_part = sb_ref[...].astype(BF16)
    lane = lax.broadcasted_iota(jnp.int32, (16, 128), 1)
    tag = jnp.where(lane == 0, a[0], jnp.where(lane == 1, a[1], a[2])).astype(F32).astype(BF16)
    out_ref[0:512, :] = a_part
    out_ref[512:768, :] = b_part
    out_ref[768:784, :] = tag
    for copy in range(XN):
        all_ref[copy, 0:512, :] = a_part
        all_ref[copy, 512:768, :] = b_part
        all_ref[copy, 768:784, :] = tag


def stage_kernel(*refs):
    half = len(refs) // 3
    copies = [
        pltpu.make_async_copy(refs[k], refs[half + k], refs[2 * half + k]) for k in range(half)
    ]
    for copy in copies:
        copy.start()
    for copy in copies:
        copy.wait()


def blocks_of(tag_row):
    row = tag_row.astype(F32)
    lane = lax.broadcasted_iota(jnp.int32, row.shape, 1)
    return [jnp.sum(jnp.where(lane == t, row, 0.0)).astype(jnp.int32) for t in range(NT)]


NT_DIMS = (((1,), (1,)), ((), ()))


def spread_lanes(block_ref, lead=()):
    a_part = block_ref[lead + (slice(0, 512), slice(None))]
    b_part = block_ref[lead + (slice(512, 768), slice(None))]
    low = (lax.broadcasted_iota(jnp.int32, (1, 128), 1) < 64).astype(F32)
    lo = jnp.concatenate([a_part[0:256], b_part * low.astype(BF16)], axis=1)
    hi = jnp.concatenate([a_part[256:512], b_part * (1.0 - low).astype(BF16)], axis=1)
    return jnp.concatenate([lo, hi], axis=0)


def by_orbital(value):
    return jnp.concatenate([value[i * BF : (i + 1) * BF] for i in range(OSUP)], axis=1)


def tags_of(block_ref, lead=()):
    return blocks_of(block_ref[lead + (slice(768, 784), slice(None))][0:1])


def rows_of(columns_ref, rows, lanes):
    return jnp.concatenate([columns_ref[p, :, lanes] for p in (rows[0], rows[1], rows[2], rows[2])], axis=0)


def columns_kernel(window_ref, metric_ref, columns_ref):
    low = lax.broadcasted_iota(jnp.int32, (AB, 128), 1) < 64
    for x in range(XN):
        cols = blocks_of(window_ref[x, 2, :, 0:128][0:1])
        lanes = [pl.ds(pl.multiple_of((q // 2) * 128, 128), 128) for q in cols]
        for p in range(AUXR // AB):
            part = [metric_ref[p, :, lane].astype(F32) for lane in lanes]
            first = pltpu.roll(part[0], 64 * (cols[0] % 2), 1)
            second = pltpu.roll(part[1], 64 * (1 - cols[1] % 2), 1)
            columns_ref[p, :, x * 256 : x * 256 + 128] = jnp.where(low, first, second).astype(BF16)
            third = pltpu.roll(part[2], 64 * (cols[2] % 2), 1)
            third = jnp.where(low, third, pltpu.roll(third, 64, 1))
            columns_ref[p, :, x * 256 + 128 : x * 256 + 256] = third.astype(BF16)


def early_kernel(group_ref, all_ref, columns_ref, out_ref):
    tags = [tags_of(all_ref, (x,)) for x in range(XN)]
    me = group_ref[0] % XN
    own = by_orbital(spread_lanes(all_ref, (me,)))
    lanes = pl.ds(pl.multiple_of(me * 256, 256), 256)
    fitted = []
    for x in range(XN):
        weights = rows_of(columns_ref, tags[x], lanes)
        rows = jnp.dot(spread_lanes(all_ref, (x,)), weights, preferred_element_type=F32)
        fitted.append(by_orbital(rows.astype(BF16)))
    fitted = jnp.concatenate(fitted, axis=0)
    out_ref[...] = lax.dot_general(own, fitted, NT_DIMS, preferred_element_type=F32)


def late_kernel(far_ref, all_ref, columns_ref, out_ref):
    weights = rows_of(columns_ref, tags_of(far_ref), slice(None))
    rows = jnp.dot(spread_lanes(far_ref), weights, preferred_element_type=F32).astype(BF16)
    for x in range(XN):
        fitted = by_orbital(rows[:, x * 256 : (x + 1) * 256])
        mine = by_orbital(spread_lanes(all_ref, (x,)))
        block = lax.dot_general(mine, fitted, NT_DIMS, preferred_element_type=F32)
        out_ref[x] = jnp.concatenate([block[0:32], block[32:64]], axis=1)


def join_kernel(group_ref, early_ref, late_ref, out_ref):
    high = group_ref[0] >= XN
    late = jnp.concatenate(
        [
            jnp.concatenate([late_ref[x][:, 0:64] for x in range(XN)], axis=1),
            jnp.concatenate([late_ref[x][:, 64:128] for x in range(XN)], axis=1),
        ],
        axis=0,
    )
    early = early_ref[...]
    out_ref[:, 0:256] = jnp.where(high, late, early)
    out_ref[:, 256:512] = jnp.where(high, early, late)


def smem():
    return pl.BlockSpec(memory_space=pltpu.SMEM)


def vmem():
    return pl.BlockSpec(memory_space=pltpu.VMEM)


def in_hbm(value):
    return pltpu.with_memory_space_constraint(value, pltpu.HBM)


def in_vmem(value):
    return pltpu.with_memory_space_constraint(value, pltpu.VMEM)


def staged(parts):
    return pl.pallas_call(
        stage_kernel,
        out_shape=[pltpu.VMEM(p.shape, p.dtype) for p in parts],
        in_specs=[pl.BlockSpec(memory_space=pltpu.HBM)] * len(parts),
        out_specs=[vmem()] * len(parts),
        scratch_shapes=[pltpu.SemaphoreType.DMA] * len(parts),
        compiler_params=pltpu.CompilerParams(vmem_limit_bytes=16 * 2**20),
    )(*[in_hbm(p) for p in parts])


def per_device(occupied, integrals, metric_inv, pattern, support):
    regions = lax.axis_size("blk")
    axes = ("blk", "grp")
    groups = [list(range(XN)), list(range(XN, 2 * XN))]
    region = lax.axis_index("blk").astype(jnp.int32).reshape(1)
    group = lax.axis_index("grp").astype(jnp.int32).reshape(1)

    def spread(value):
        value = jnp.broadcast_to(value[None], (XN,) + value.shape)
        return lax.all_to_all(value, "grp", 0, 0, axis_index_groups=groups)

    pairs = [swap_pairs(j, regions, 8) for j in range(2)]
    asked = []
    for j in range(2):
        asked.append(lax.ppermute(support, axes, pairs[j]))
    (occupied,) = staged([occupied])
    (integrals,) = staged([integrals])
    asked = jnp.concatenate(asked, axis=1)[0]
    wanted = asked[:, None] == jnp.arange(occupied.shape[1], dtype=jnp.int32)[None, :]
    answer = lax.dot_general(wanted.astype(BF16), occupied, NT_DIMS, preferred_element_type=F32)
    answer = answer.astype(BF16)
    answers = []
    for j in range(2):
        answers.append(lax.ppermute(answer[j * OSUP : (j + 1) * OSUP], axes, pairs[j]))
    tag = jnp.pad(pattern[0, 0, :, 2].astype(BF16), (0, occupied.shape[0] - NT))
    answers.append(jnp.broadcast_to(tag, (OSUP, occupied.shape[0])))
    window = spread(jnp.stack(answers, 0))

    message, copies = pl.pallas_call(
        contribution_kernel,
        out_shape=[
            pltpu.VMEM((ROWS, 128), BF16),
            jax.ShapeDtypeStruct((XN, ROWS, 128), BF16),
        ],
        in_specs=[smem(), smem(), vmem(), vmem()],
        out_specs=[vmem(), vmem()],
        scratch_shapes=[pltpu.VMEM((512, 128), F32), pltpu.VMEM((256, 128), F32)],
        name="contribution",
            compiler_params=pltpu.CompilerParams(vmem_limit_bytes=16 * 2**20),
    )(region, pattern, in_vmem(window), in_vmem(integrals))

    far = lax.ppermute(message, "grp", [(g, (g + XN) % (2 * XN)) for g in range(2 * XN)])
    everyone = lax.all_to_all(copies, "grp", 0, 0, axis_index_groups=groups)
    limit = pltpu.CompilerParams(vmem_limit_bytes=24 * 2**20)
    columns = pl.pallas_call(
        columns_kernel,
        out_shape=pltpu.VMEM((AUXR // AB, AB, XN * 256), BF16),
        in_specs=[vmem(), vmem()],
        out_specs=vmem(),
        compiler_params=limit,
        name="columns",
    )(in_vmem(window), in_hbm(metric_inv.reshape(AUXR // AB, AB, AUXR)))
    early = pl.pallas_call(
        early_kernel,
        out_shape=pltpu.VMEM((BF, XN * BF), F32),
        in_specs=[smem(), vmem(), vmem()],
        out_specs=vmem(),
        compiler_params=limit,
        name="early",
    )(group, in_vmem(everyone), in_vmem(columns))
    late = pl.pallas_call(
        late_kernel,
        out_shape=pltpu.VMEM((XN, BF // 2, 2 * BF), F32),
        in_specs=[vmem(), vmem(), vmem()],
        out_specs=vmem(),
        compiler_params=limit,
        name="late",
    )(in_vmem(far), in_vmem(everyone), in_vmem(columns))
    late = lax.all_to_all(late, "grp", 0, 0, axis_index_groups=groups)
    return pl.pallas_call(
        join_kernel,
        out_shape=jax.ShapeDtypeStruct((BF, 2 * XN * BF), F32),
        in_specs=[smem(), vmem(), vmem()],
        out_specs=vmem(),
        name="join",
            compiler_params=pltpu.CompilerParams(vmem_limit_bytes=16 * 2**20),
    )(group, in_vmem(early), in_vmem(late))


def solution(mesh):
    placed = (
        P("blk", None),
        P("blk", "grp", None, None, None),
        P("blk", None),
        P("blk", "grp", None, None),
        P("blk", None),
    )
    return jax.shard_map(
        per_device, mesh=mesh, in_specs=placed, out_specs=P(("blk", "grp"), None), check_vma=False
    )
```

```python
import jax
import jax.numpy as jnp
from jax import lax
from jax.experimental import pallas as pl
from jax.experimental.pallas import tpu as pltpu
from jax.sharding import PartitionSpec as P


BF = 64
AB = 64
AUXR = 1024
OSUP = 8
NT = 3
REACH = 3
XN = 4
DATA = OSUP * BF * NT * AB // 128
ROWS = DATA + 16
F32 = jnp.float32
BF16 = jnp.bfloat16


TASKS = (((3, 0), (3, 1), (1, 1), (2, 1)), ((1, 0), (0, 0), (2, 0), (0, 0)))


def swap_pairs(j, regions, zlo):
    pairs = []
    for region in range(regions):
        for group in range(2 * XN):
            distance, phase = TASKS[j][group % XN]
            place = (region // 2 if distance == 2 else region) + phase
            target = region + (distance if place % 2 == 0 else -distance)
            z = (group // XN) * zlo + (region // 2) % zlo + target // 2 - region // 2
            copy = (z % (2 * zlo)) // zlo * XN + group % XN
            pairs.append((region * 2 * XN + group, (target % regions) * 2 * XN + copy))
    return pairs


def contribution_kernel(region_ref, pattern_ref, window_ref, integrals_ref, out_ref, sa_ref, sb_ref):
    region = region_ref[0]
    a = [pattern_ref[4 * t + 2] for t in range(NT)]
    live = [pattern_ref[4 * t + 3] for t in range(NT)]
    lane8 = lax.broadcasted_iota(jnp.int32, (OSUP, 128), 1)
    low8 = lane8 < 64

    def tile(t, want_high):
        source = pattern_ref[4 * t + 0]
        offset = (source - region + 64 + REACH) % 64 - REACH
        distance = jnp.abs(offset)
        place = jnp.where(distance == 2, region // 2, region) % 2
        phase = jnp.where(offset > 0, place, 1 - place)
        x = jnp.where(distance == 3, phase, jnp.where(distance == 0, 1, 2 * phase))
        x = jnp.where(distance == 2, 2 + phase, x)
        first = jnp.where(distance == 1, phase, jnp.where(distance == 2, phase, distance // 3))
        j = 1 - first
        m = pattern_ref[4 * t + 1]
        lanes = pl.ds(pl.multiple_of((m // 2) * 128, 128), 128)
        part = window_ref[x, j, :, lanes].astype(F32)
        return pltpu.roll(part, 64 * ((m % 2) ^ want_high), 1)

    chunk0 = jnp.where(low8, tile(0, 0), tile(1, 1))
    chunk1 = tile(2, 0)[:, :64]
    rep = [jnp.int32(0)]
    rep.append(jnp.where(a[1] == a[0], 0, 1))
    rep.append(jnp.where(a[2] == a[0], 0, jnp.where(a[2] == a[1], 1, 2)))
    rows = []
    for t in range(NT):
        w = [jnp.where(rep[u] == t, live[u], 0).astype(F32) for u in range(NT)]
        first = chunk0 * jnp.where(low8, w[0], w[1])
        rows.append(jnp.concatenate([first, chunk1 * w[2]], axis=1))
    lhs = jnp.concatenate(rows, axis=0).astype(BF16)
    tiles = integrals_ref[0, 0].reshape(NT * BF, BF * AB)
    c = jnp.dot(lhs, tiles, preferred_element_type=F32)
    for k in range(BF * AB // 128):
        v = [c[t * 8 : (t + 1) * 8, k * 128 : (k + 1) * 128] for t in range(NT)]
        s0, s1, s2 = [pltpu.roll(u, 64, 1) for u in v]
        half = pltpu.roll(v[2], 4, 0)
        half_s = pltpu.roll(s2, 4, 0)
        sa_ref[pl.ds(2 * k, OSUP, stride=BF), :] = jnp.where(low8, v[0], s1)
        sa_ref[pl.ds(2 * k + 1, OSUP, stride=BF), :] = jnp.where(low8, s0, v[1])
        sb_ref[pl.ds(2 * k, OSUP // 2, stride=BF), :] = jnp.where(low8, v[2], half_s)[: OSUP // 2]
        sb_ref[pl.ds(2 * k + 1, OSUP // 2, stride=BF), :] = jnp.where(low8, s2, half)[: OSUP // 2]
    a_part = sa_ref[...].astype(BF16)
    b_part = sb_ref[...].astype(BF16)
    lane = lax.broadcasted_iota(jnp.int32, (16, 128), 1)
    tag = jnp.where(lane == 0, a[0], jnp.where(lane == 1, a[1], a[2])).astype(F32).astype(BF16)
    out_ref[0:512, :] = a_part
    out_ref[512:768, :] = b_part
    out_ref[768:784, :] = tag


def stage_kernel(*refs):
    half = len(refs) // 3
    copies = [
        pltpu.make_async_copy(refs[k], refs[half + k], refs[2 * half + k]) for k in range(half)
    ]
    for copy in copies:
        copy.start()
    for copy in copies:
        copy.wait()


def blocks_of(tag_row):
    row = tag_row.astype(F32)
    lane = lax.broadcasted_iota(jnp.int32, row.shape, 1)
    return [jnp.sum(jnp.where(lane == t, row, 0.0)).astype(jnp.int32) for t in range(NT)]


NT_DIMS = (((1,), (1,)), ((), ()))


def spread_lanes(block_ref, lead=()):
    a_part = block_ref[lead + (slice(0, 512), slice(None))]
    b_part = block_ref[lead + (slice(512, 768), slice(None))]
    low = (lax.broadcasted_iota(jnp.int32, (1, 128), 1) < 64).astype(F32)
    lo = jnp.concatenate([a_part[0:256], b_part * low.astype(BF16)], axis=1)
    hi = jnp.concatenate([a_part[256:512], b_part * (1.0 - low).astype(BF16)], axis=1)
    return jnp.concatenate([lo, hi], axis=0)


def by_orbital(value):
    return jnp.concatenate([value[i * BF : (i + 1) * BF] for i in range(OSUP)], axis=1)


def tags_of(block_ref, lead=()):
    return blocks_of(block_ref[lead + (slice(768, 784), slice(None))][0:1])


def rows_of(columns_ref, rows, lanes):
    return jnp.concatenate([columns_ref[p, :, lanes] for p in (rows[0], rows[1], rows[2], rows[2])], axis=0)


def columns_kernel(window_ref, metric_ref, columns_ref):
    low = lax.broadcasted_iota(jnp.int32, (AB, 128), 1) < 64
    for x in range(XN):
        cols = blocks_of(window_ref[x, 2, :, 0:128][0:1])
        lanes = [pl.ds(pl.multiple_of((q // 2) * 128, 128), 128) for q in cols]
        for p in range(AUXR // AB):
            part = [metric_ref[p, :, lane].astype(F32) for lane in lanes]
            first = pltpu.roll(part[0], 64 * (cols[0] % 2), 1)
            second = pltpu.roll(part[1], 64 * (1 - cols[1] % 2), 1)
            columns_ref[p, :, x * 256 : x * 256 + 128] = jnp.where(low, first, second).astype(BF16)
            third = pltpu.roll(part[2], 64 * (cols[2] % 2), 1)
            third = jnp.where(low, third, pltpu.roll(third, 64, 1))
            columns_ref[p, :, x * 256 + 128 : x * 256 + 256] = third.astype(BF16)


def early_kernel(group_ref, all_ref, columns_ref, out_ref):
    tags = [tags_of(all_ref, (x,)) for x in range(XN)]
    me = group_ref[0] % XN
    own = by_orbital(spread_lanes(all_ref, (me,)))
    lanes = pl.ds(pl.multiple_of(me * 256, 256), 256)
    fitted = []
    for x in range(XN):
        weights = rows_of(columns_ref, tags[x], lanes)
        rows = jnp.dot(spread_lanes(all_ref, (x,)), weights, preferred_element_type=F32)
        fitted.append(by_orbital(rows.astype(BF16)))
    fitted = jnp.concatenate(fitted, axis=0)
    out_ref[...] = lax.dot_general(own, fitted, NT_DIMS, preferred_element_type=F32)


def late_kernel(far_ref, all_ref, columns_ref, out_ref):
    weights = rows_of(columns_ref, tags_of(far_ref), slice(None))
    rows = jnp.dot(spread_lanes(far_ref), weights, preferred_element_type=F32).astype(BF16)
    for x in range(XN):
        fitted = by_orbital(rows[:, x * 256 : (x + 1) * 256])
        mine = by_orbital(spread_lanes(all_ref, (x,)))
        block = lax.dot_general(mine, fitted, NT_DIMS, preferred_element_type=F32)
        out_ref[x] = jnp.concatenate([block[0:32], block[32:64]], axis=1)


def join_kernel(group_ref, early_ref, late_ref, out_ref):
    high = group_ref[0] >= XN
    late = jnp.concatenate(
        [
            jnp.concatenate([late_ref[x][:, 0:64] for x in range(XN)], axis=1),
            jnp.concatenate([late_ref[x][:, 64:128] for x in range(XN)], axis=1),
        ],
        axis=0,
    )
    early = early_ref[...]
    out_ref[:, 0:256] = jnp.where(high, late, early)
    out_ref[:, 256:512] = jnp.where(high, early, late)


def smem():
    return pl.BlockSpec(memory_space=pltpu.SMEM)


def vmem():
    return pl.BlockSpec(memory_space=pltpu.VMEM)


def in_hbm(value):
    return pltpu.with_memory_space_constraint(value, pltpu.HBM)


def in_vmem(value):
    return pltpu.with_memory_space_constraint(value, pltpu.VMEM)


def staged(parts):
    return pl.pallas_call(
        stage_kernel,
        out_shape=[pltpu.VMEM(p.shape, p.dtype) for p in parts],
        in_specs=[pl.BlockSpec(memory_space=pltpu.HBM)] * len(parts),
        out_specs=[vmem()] * len(parts),
        scratch_shapes=[pltpu.SemaphoreType.DMA] * len(parts),
        compiler_params=pltpu.CompilerParams(vmem_limit_bytes=16 * 2**20),
    )(*[in_hbm(p) for p in parts])


def per_device(occupied, integrals, metric_inv, pattern, support):
    regions = lax.axis_size("blk")
    axes = ("blk", "grp")
    groups = [list(range(XN)), list(range(XN, 2 * XN))]
    region = lax.axis_index("blk").astype(jnp.int32).reshape(1)
    group = lax.axis_index("grp").astype(jnp.int32).reshape(1)

    def spread(value):
        value = jnp.broadcast_to(value[None], (XN,) + value.shape)
        return lax.all_to_all(value, "grp", 0, 0, axis_index_groups=groups)

    pairs = [swap_pairs(j, regions, 8) for j in range(2)]
    asked = []
    for j in range(2):
        asked.append(lax.ppermute(support, axes, pairs[j]))
    (occupied,) = staged([occupied])
    (integrals,) = staged([integrals])
    asked = jnp.concatenate(asked, axis=1)[0]
    wanted = asked[:, None] == jnp.arange(occupied.shape[1], dtype=jnp.int32)[None, :]
    answer = lax.dot_general(wanted.astype(BF16), occupied, NT_DIMS, preferred_element_type=F32)
    answer = answer.astype(BF16)
    answers = []
    for j in range(2):
        answers.append(lax.ppermute(answer[j * OSUP : (j + 1) * OSUP], axes, pairs[j]))
    tag = jnp.pad(pattern[0, 0, :, 2].astype(BF16), (0, occupied.shape[0] - NT))
    answers.append(jnp.broadcast_to(tag, (OSUP, occupied.shape[0])))
    stacked, slots, region = lax.optimization_barrier((jnp.stack(answers, 0), pattern.reshape(-1), region))
    window = spread(stacked)

    message = pl.pallas_call(
        contribution_kernel,
        out_shape=pltpu.VMEM((ROWS, 128), BF16),
        in_specs=[smem(), smem(), vmem(), vmem()],
        out_specs=vmem(),
        scratch_shapes=[pltpu.VMEM((512, 128), F32), pltpu.VMEM((256, 128), F32)],
        name="contribution",
            compiler_params=pltpu.CompilerParams(vmem_limit_bytes=16 * 2**20),
    )(region, slots, in_vmem(window), in_vmem(integrals))

    far = lax.ppermute(message, "grp", [(g, (g + XN) % (2 * XN)) for g in range(2 * XN)])
    everyone = spread(message)
    limit = pltpu.CompilerParams(vmem_limit_bytes=24 * 2**20)
    columns = pl.pallas_call(
        columns_kernel,
        out_shape=pltpu.VMEM((AUXR // AB, AB, XN * 256), BF16),
        in_specs=[vmem(), vmem()],
        out_specs=vmem(),
        compiler_params=limit,
        name="columns",
    )(in_vmem(window), in_hbm(metric_inv.reshape(AUXR // AB, AB, AUXR)))
    early = pl.pallas_call(
        early_kernel,
        out_shape=pltpu.VMEM((BF, XN * BF), F32),
        in_specs=[smem(), vmem(), vmem()],
        out_specs=vmem(),
        compiler_params=limit,
        name="early",
    )(group, in_vmem(everyone), in_vmem(columns))
    late = pl.pallas_call(
        late_kernel,
        out_shape=pltpu.VMEM((XN, BF // 2, 2 * BF), F32),
        in_specs=[vmem(), vmem(), vmem()],
        out_specs=vmem(),
        compiler_params=limit,
        name="late",
    )(in_vmem(far), in_vmem(everyone), in_vmem(columns))
    late = lax.all_to_all(late, "grp", 0, 0, axis_index_groups=groups)
    return pl.pallas_call(
        join_kernel,
        out_shape=jax.ShapeDtypeStruct((BF, 2 * XN * BF), F32),
        in_specs=[smem(), vmem(), vmem()],
        out_specs=vmem(),
        name="join",
            compiler_params=pltpu.CompilerParams(vmem_limit_bytes=16 * 2**20),
    )(group, in_vmem(early), in_vmem(late))


def solution(mesh):
    placed = (
        P("blk", None),
        P("blk", "grp", None, None, None),
        P("blk", None),
        P("blk", "grp", None, None),
        P("blk", None),
    )
    return jax.shard_map(per_device, mesh=mesh, in_specs=placed, out_specs=P(("blk", "grp"), None), check_vma=False)
```

```python
import jax
import jax.numpy as jnp
from jax import lax
from jax.experimental import pallas as pl
from jax.experimental.pallas import tpu as pltpu
from jax.sharding import PartitionSpec as P


BF = 64
AB = 64
AUXR = 1024
OSUP = 8
NT = 3
REACH = 3
XN = 4
DATA = OSUP * BF * NT * AB // 128
ROWS = DATA + 8
F32 = jnp.float32
BF16 = jnp.bfloat16


TASKS = (((3, 0), (3, 1), (1, 1), (2, 1)), ((1, 0), (0, 0), (2, 0), (0, 0)))


def swap_pairs(j, regions, zlo):
    pairs = []
    for region in range(regions):
        for group in range(2 * XN):
            distance, phase = TASKS[j][group % XN]
            place = (region // 2 if distance == 2 else region) + phase
            target = region + (distance if place % 2 == 0 else -distance)
            z = (group // XN) * zlo + (region // 2) % zlo + target // 2 - region // 2
            copy = (z % (2 * zlo)) // zlo * XN + group % XN
            pairs.append((region * 2 * XN + group, (target % regions) * 2 * XN + copy))
    return pairs


def contribution_kernel(region_ref, pattern_ref, window_ref, integrals_ref, out_ref, sa_ref, sb_ref):
    region = region_ref[0]
    a = [pattern_ref[4 * t + 2] for t in range(NT)]
    live = [pattern_ref[4 * t + 3] for t in range(NT)]
    lane8 = lax.broadcasted_iota(jnp.int32, (OSUP, 128), 1)
    low8 = lane8 < 64

    def tile(t, want_high):
        source = pattern_ref[4 * t + 0]
        offset = (source - region + 64 + REACH) % 64 - REACH
        distance = jnp.abs(offset)
        place = jnp.where(distance == 2, region // 2, region) % 2
        phase = jnp.where(offset > 0, place, 1 - place)
        x = jnp.where(distance == 3, phase, jnp.where(distance == 0, 1, 2 * phase))
        x = jnp.where(distance == 2, 2 + phase, x)
        first = jnp.where(distance == 1, phase, jnp.where(distance == 2, phase, distance // 3))
        j = 1 - first
        m = pattern_ref[4 * t + 1]
        lanes = pl.ds(pl.multiple_of((m // 2) * 128, 128), 128)
        part = window_ref[x, j, :, lanes].astype(F32)
        return pltpu.roll(part, 64 * ((m % 2) ^ want_high), 1)

    chunk0 = jnp.where(low8, tile(0, 0), tile(1, 1))
    chunk1 = tile(2, 0)[:, :64]
    rep = [jnp.int32(0)]
    rep.append(jnp.where(a[1] == a[0], 0, 1))
    rep.append(jnp.where(a[2] == a[0], 0, jnp.where(a[2] == a[1], 1, 2)))
    rows = []
    for t in range(NT):
        w = [jnp.where(rep[u] == t, live[u], 0).astype(F32) for u in range(NT)]
        first = chunk0 * jnp.where(low8, w[0], w[1])
        rows.append(jnp.concatenate([first, chunk1 * w[2]], axis=1))
    lhs = jnp.concatenate(rows, axis=0).astype(BF16)
    tiles = integrals_ref[0, 0].reshape(NT * BF, BF * AB)
    c = jnp.dot(lhs, tiles, preferred_element_type=F32)
    for k in range(BF * AB // 128):
        v = [c[t * 8 : (t + 1) * 8, k * 128 : (k + 1) * 128] for t in range(NT)]
        s0, s1, s2 = [pltpu.roll(u, 64, 1) for u in v]
        half = pltpu.roll(v[2], 4, 0)
        half_s = pltpu.roll(s2, 4, 0)
        sa_ref[pl.ds(2 * k, OSUP, stride=BF), :] = jnp.where(low8, v[0], s1)
        sa_ref[pl.ds(2 * k + 1, OSUP, stride=BF), :] = jnp.where(low8, s0, v[1])
        sb_ref[pl.ds(2 * k, OSUP // 2, stride=BF), :] = jnp.where(low8, v[2], half_s)[: OSUP // 2]
        sb_ref[pl.ds(2 * k + 1, OSUP // 2, stride=BF), :] = jnp.where(low8, s2, half)[: OSUP // 2]
    a_part = sa_ref[...].astype(BF16)
    b_part = sb_ref[...].astype(BF16)
    lane = lax.broadcasted_iota(jnp.int32, (8, 128), 1)
    tag = jnp.where(lane == 0, a[0], jnp.where(lane == 1, a[1], a[2])).astype(F32).astype(BF16)
    out_ref[0:512, :] = a_part
    out_ref[512:768, :] = b_part
    out_ref[768:776, :] = tag


def stage_kernel(*refs):
    half = len(refs) // 3
    copies = [
        pltpu.make_async_copy(refs[k], refs[half + k], refs[2 * half + k]) for k in range(half)
    ]
    for copy in copies:
        copy.start()
    for copy in copies:
        copy.wait()


def blocks_of(tag_row):
    row = tag_row.astype(F32)
    lane = lax.broadcasted_iota(jnp.int32, row.shape, 1)
    return [jnp.sum(jnp.where(lane == t, row, 0.0)).astype(jnp.int32) for t in range(NT)]


NT_DIMS = (((1,), (1,)), ((), ()))


def spread_lanes(block_ref, lead=()):
    a_part = block_ref[lead + (slice(0, 512), slice(None))]
    b_part = block_ref[lead + (slice(512, 768), slice(None))]
    low = (lax.broadcasted_iota(jnp.int32, (1, 128), 1) < 64).astype(F32)
    lo = jnp.concatenate([a_part[0:256], b_part * low.astype(BF16)], axis=1)
    hi = jnp.concatenate([a_part[256:512], b_part * (1.0 - low).astype(BF16)], axis=1)
    return jnp.concatenate([lo, hi], axis=0)


def by_orbital(value):
    return jnp.concatenate([value[i * BF : (i + 1) * BF] for i in range(OSUP)], axis=1)


def tags_of(block_ref, lead=()):
    return blocks_of(block_ref[lead + (slice(768, 776), slice(None))][0:1])


def rows_of(columns_ref, rows, lanes):
    return jnp.concatenate([columns_ref[p, :, lanes] for p in (rows[0], rows[1], rows[2], rows[2])], axis=0)


def columns_kernel(window_ref, metric_ref, columns_ref):
    low = lax.broadcasted_iota(jnp.int32, (AB, 128), 1) < 64
    for x in range(XN):
        cols = blocks_of(window_ref[x, 2, :, 0:128][0:1])
        lanes = [pl.ds(pl.multiple_of((q // 2) * 128, 128), 128) for q in cols]
        for p in range(AUXR // AB):
            part = [metric_ref[p, :, lane].astype(F32) for lane in lanes]
            first = pltpu.roll(part[0], 64 * (cols[0] % 2), 1)
            second = pltpu.roll(part[1], 64 * (1 - cols[1] % 2), 1)
            columns_ref[p, :, x * 256 : x * 256 + 128] = jnp.where(low, first, second).astype(BF16)
            third = pltpu.roll(part[2], 64 * (cols[2] % 2), 1)
            third = jnp.where(low, third, pltpu.roll(third, 64, 1))
            columns_ref[p, :, x * 256 + 128 : x * 256 + 256] = third.astype(BF16)


def early_kernel(group_ref, all_ref, columns_ref, out_ref):
    tags = [tags_of(all_ref, (x,)) for x in range(XN)]
    me = group_ref[0] % XN
    own = by_orbital(spread_lanes(all_ref, (me,)))
    lanes = pl.ds(pl.multiple_of(me * 256, 256), 256)
    fitted = []
    for x in range(XN):
        weights = rows_of(columns_ref, tags[x], lanes)
        rows = jnp.dot(spread_lanes(all_ref, (x,)), weights, preferred_element_type=F32)
        fitted.append(by_orbital(rows.astype(BF16)))
    fitted = jnp.concatenate(fitted, axis=0)
    out_ref[...] = lax.dot_general(own, fitted, NT_DIMS, preferred_element_type=F32)


def late_kernel(far_ref, all_ref, columns_ref, out_ref):
    weights = rows_of(columns_ref, tags_of(far_ref), slice(None))
    rows = jnp.dot(spread_lanes(far_ref), weights, preferred_element_type=F32).astype(BF16)
    for x in range(XN):
        fitted = by_orbital(rows[:, x * 256 : (x + 1) * 256])
        mine = by_orbital(spread_lanes(all_ref, (x,)))
        block = lax.dot_general(mine, fitted, NT_DIMS, preferred_element_type=F32)
        out_ref[x] = jnp.concatenate([block[0:32], block[32:64]], axis=1)


def join_kernel(group_ref, early_ref, late_ref, out_ref):
    high = group_ref[0] >= XN
    late = jnp.concatenate(
        [
            jnp.concatenate([late_ref[x][:, 0:64] for x in range(XN)], axis=1),
            jnp.concatenate([late_ref[x][:, 64:128] for x in range(XN)], axis=1),
        ],
        axis=0,
    )
    early = early_ref[...]
    out_ref[:, 0:256] = jnp.where(high, late, early)
    out_ref[:, 256:512] = jnp.where(high, early, late)


def smem():
    return pl.BlockSpec(memory_space=pltpu.SMEM)


def vmem():
    return pl.BlockSpec(memory_space=pltpu.VMEM)


def in_hbm(value):
    return pltpu.with_memory_space_constraint(value, pltpu.HBM)


def in_vmem(value):
    return pltpu.with_memory_space_constraint(value, pltpu.VMEM)


def staged(parts):
    return pl.pallas_call(
        stage_kernel,
        out_shape=[pltpu.VMEM(p.shape, p.dtype) for p in parts],
        in_specs=[pl.BlockSpec(memory_space=pltpu.HBM)] * len(parts),
        out_specs=[vmem()] * len(parts),
        scratch_shapes=[pltpu.SemaphoreType.DMA] * len(parts),
        compiler_params=pltpu.CompilerParams(vmem_limit_bytes=16 * 2**20),
    )(*[in_hbm(p) for p in parts])


def per_device(occupied, integrals, metric_inv, pattern, support):
    regions = lax.axis_size("blk")
    axes = ("blk", "grp")
    groups = [list(range(XN)), list(range(XN, 2 * XN))]
    region = lax.axis_index("blk").astype(jnp.int32).reshape(1)
    group = lax.axis_index("grp").astype(jnp.int32).reshape(1)

    def spread(value):
        value = jnp.broadcast_to(value[None], (XN,) + value.shape)
        return lax.all_to_all(value, "grp", 0, 0, axis_index_groups=groups)

    pairs = [swap_pairs(j, regions, 8) for j in range(2)]
    asked = []
    for j in range(2):
        asked.append(lax.ppermute(support, axes, pairs[j]))
    (occupied,) = staged([occupied])
    (integrals,) = staged([integrals])
    asked = jnp.concatenate(asked, axis=1)[0]
    wanted = asked[:, None] == jnp.arange(occupied.shape[1], dtype=jnp.int32)[None, :]
    answer = lax.dot_general(wanted.astype(BF16), occupied, NT_DIMS, preferred_element_type=F32)
    answer = answer.astype(BF16)
    answers = []
    for j in range(2):
        answers.append(lax.ppermute(answer[j * OSUP : (j + 1) * OSUP], axes, pairs[j]))
    tag = jnp.pad(pattern[0, 0, :, 2].astype(BF16), (0, occupied.shape[0] - NT))
    answers.append(jnp.broadcast_to(tag, (OSUP, occupied.shape[0])))
    stacked, slots, region = lax.optimization_barrier((jnp.stack(answers, 0), pattern.reshape(-1), region))
    window = spread(stacked)

    message = pl.pallas_call(
        contribution_kernel,
        out_shape=pltpu.VMEM((ROWS, 128), BF16),
        in_specs=[smem(), smem(), vmem(), vmem()],
        out_specs=vmem(),
        scratch_shapes=[pltpu.VMEM((512, 128), F32), pltpu.VMEM((256, 128), F32)],
        name="contribution",
            compiler_params=pltpu.CompilerParams(vmem_limit_bytes=16 * 2**20),
    )(region, slots, in_vmem(window), in_vmem(integrals))

    far = lax.ppermute(message, "grp", [(g, (g + XN) % (2 * XN)) for g in range(2 * XN)])
    everyone = spread(message)
    limit = pltpu.CompilerParams(vmem_limit_bytes=24 * 2**20)
    columns = pl.pallas_call(
        columns_kernel,
        out_shape=pltpu.VMEM((AUXR // AB, AB, XN * 256), BF16),
        in_specs=[vmem(), vmem()],
        out_specs=vmem(),
        compiler_params=limit,
        name="columns",
    )(in_vmem(window), in_hbm(metric_inv.reshape(AUXR // AB, AB, AUXR)))
    early = pl.pallas_call(
        early_kernel,
        out_shape=pltpu.VMEM((BF, XN * BF), F32),
        in_specs=[smem(), vmem(), vmem()],
        out_specs=vmem(),
        compiler_params=limit,
        name="early",
    )(group, in_vmem(everyone), in_vmem(columns))
    late = pl.pallas_call(
        late_kernel,
        out_shape=pltpu.VMEM((XN, BF // 2, 2 * BF), F32),
        in_specs=[vmem(), vmem(), vmem()],
        out_specs=vmem(),
        compiler_params=limit,
        name="late",
    )(in_vmem(far), in_vmem(everyone), in_vmem(columns))
    late = lax.all_to_all(late, "grp", 0, 0, axis_index_groups=groups)
    return pl.pallas_call(
        join_kernel,
        out_shape=jax.ShapeDtypeStruct((BF, 2 * XN * BF), F32),
        in_specs=[smem(), vmem(), vmem()],
        out_specs=vmem(),
        name="join",
            compiler_params=pltpu.CompilerParams(vmem_limit_bytes=16 * 2**20),
    )(group, in_vmem(early), in_vmem(late))


def solution(mesh):
    placed = (
        P("blk", None),
        P("blk", "grp", None, None, None),
        P("blk", None),
        P("blk", "grp", None, None),
        P("blk", None),
    )
    return jax.shard_map(per_device, mesh=mesh, in_specs=placed, out_specs=P(("blk", "grp"), None), check_vma=False)
```

```python
import jax
import jax.numpy as jnp
from jax import lax
from jax.experimental import pallas as pl
from jax.experimental.pallas import tpu as pltpu
from jax.sharding import PartitionSpec as P


BF = 64
AB = 64
AUXR = 1024
OSUP = 8
NT = 3
REACH = 3
XN = 4
DATA = OSUP * BF * NT * AB // 128
ROWS = DATA + 8
F32 = jnp.float32
BF16 = jnp.bfloat16


TASKS = (((3, 0), (3, 1), (1, 1), (2, 1)), ((2, 0), (0, 0), (0, 0), (1, 0)))


def swap_pairs(j, regions, zlo):
    pairs = []
    for region in range(regions):
        for group in range(2 * XN):
            distance, phase = TASKS[j][group % XN]
            place = (region // 2 if distance == 2 else region) + phase
            target = region + (distance if place % 2 == 0 else -distance)
            z = (group // XN) * zlo + (region // 2) % zlo + target // 2 - region // 2
            copy = (z % (2 * zlo)) // zlo * XN + group % XN
            pairs.append((region * 2 * XN + group, (target % regions) * 2 * XN + copy))
    return pairs


def contribution_kernel(region_ref, pattern_ref, window_ref, integrals_ref, out_ref, sa_ref, sb_ref):
    region = region_ref[0]
    a = [pattern_ref[4 * t + 2] for t in range(NT)]
    live = [pattern_ref[4 * t + 3] for t in range(NT)]
    lane8 = lax.broadcasted_iota(jnp.int32, (OSUP, 128), 1)
    low8 = lane8 < 64

    def tile(t, want_high):
        source = pattern_ref[4 * t + 0]
        offset = (source - region + 64 + REACH) % 64 - REACH
        distance = jnp.abs(offset)
        place = jnp.where(distance == 2, region // 2, region) % 2
        phase = jnp.where(offset > 0, place, 1 - place)
        x = jnp.where(distance == 3, phase, jnp.where(distance == 2, 3 * phase, 3 - phase))
        x = jnp.where(distance == 0, 1, x)
        first = jnp.where(distance == 1, phase, jnp.where(distance == 2, phase, distance // 3))
        j = 1 - first
        m = pattern_ref[4 * t + 1]
        lanes = pl.ds(pl.multiple_of((m // 2) * 128, 128), 128)
        part = window_ref[x, j, :, lanes].astype(F32)
        return pltpu.roll(part, 64 * ((m % 2) ^ want_high), 1)

    chunk0 = jnp.where(low8, tile(0, 0), tile(1, 1))
    chunk1 = tile(2, 0)[:, :64]
    rep = [jnp.int32(0)]
    rep.append(jnp.where(a[1] == a[0], 0, 1))
    rep.append(jnp.where(a[2] == a[0], 0, jnp.where(a[2] == a[1], 1, 2)))
    rows = []
    for t in range(NT):
        w = [jnp.where(rep[u] == t, live[u], 0).astype(F32) for u in range(NT)]
        first = chunk0 * jnp.where(low8, w[0], w[1])
        rows.append(jnp.concatenate([first, chunk1 * w[2]], axis=1))
    lhs = jnp.concatenate(rows, axis=0).astype(BF16)
    tiles = integrals_ref[0, 0].reshape(NT * BF, BF * AB)
    c = jnp.dot(lhs, tiles, preferred_element_type=F32)
    for k in range(BF * AB // 128):
        v = [c[t * 8 : (t + 1) * 8, k * 128 : (k + 1) * 128] for t in range(NT)]
        s0, s1, s2 = [pltpu.roll(u, 64, 1) for u in v]
        half = pltpu.roll(v[2], 4, 0)
        half_s = pltpu.roll(s2, 4, 0)
        sa_ref[pl.ds(2 * k, OSUP, stride=BF), :] = jnp.where(low8, v[0], s1)
        sa_ref[pl.ds(2 * k + 1, OSUP, stride=BF), :] = jnp.where(low8, s0, v[1])
        sb_ref[pl.ds(2 * k, OSUP // 2, stride=BF), :] = jnp.where(low8, v[2], half_s)[: OSUP // 2]
        sb_ref[pl.ds(2 * k + 1, OSUP // 2, stride=BF), :] = jnp.where(low8, s2, half)[: OSUP // 2]
    a_part = sa_ref[...].astype(BF16)
    b_part = sb_ref[...].astype(BF16)
    lane = lax.broadcasted_iota(jnp.int32, (8, 128), 1)
    tag = jnp.where(lane == 0, a[0], jnp.where(lane == 1, a[1], a[2])).astype(F32).astype(BF16)
    out_ref[0:512, :] = a_part
    out_ref[512:768, :] = b_part
    out_ref[768:776, :] = tag


def stage_kernel(*refs):
    half = len(refs) // 3
    copies = [
        pltpu.make_async_copy(refs[k], refs[half + k], refs[2 * half + k]) for k in range(half)
    ]
    for copy in copies:
        copy.start()
    for copy in copies:
        copy.wait()


def blocks_of(tag_row):
    row = tag_row.astype(F32)
    lane = lax.broadcasted_iota(jnp.int32, row.shape, 1)
    return [jnp.sum(jnp.where(lane == t, row, 0.0)).astype(jnp.int32) for t in range(NT)]


NT_DIMS = (((1,), (1,)), ((), ()))


def spread_lanes(block_ref, lead=()):
    a_part = block_ref[lead + (slice(0, 512), slice(None))]
    b_part = block_ref[lead + (slice(512, 768), slice(None))]
    low = (lax.broadcasted_iota(jnp.int32, (1, 128), 1) < 64).astype(F32)
    lo = jnp.concatenate([a_part[0:256], b_part * low.astype(BF16)], axis=1)
    hi = jnp.concatenate([a_part[256:512], b_part * (1.0 - low).astype(BF16)], axis=1)
    return jnp.concatenate([lo, hi], axis=0)


def by_orbital(value):
    return jnp.concatenate([value[i * BF : (i + 1) * BF] for i in range(OSUP)], axis=1)


def tags_of(block_ref, lead=()):
    return blocks_of(block_ref[lead + (slice(768, 776), slice(None))][0:1])


def rows_of(columns_ref, rows, lanes):
    return jnp.concatenate([columns_ref[p, :, lanes] for p in (rows[0], rows[1], rows[2], rows[2])], axis=0)


def columns_kernel(window_ref, metric_ref, columns_ref):
    low = lax.broadcasted_iota(jnp.int32, (AB, 128), 1) < 64
    for x in range(XN):
        cols = blocks_of(window_ref[x, 2, :, 0:128][0:1])
        lanes = [pl.ds(pl.multiple_of((q // 2) * 128, 128), 128) for q in cols]
        for p in range(AUXR // AB):
            part = [metric_ref[p, :, lane].astype(F32) for lane in lanes]
            first = pltpu.roll(part[0], 64 * (cols[0] % 2), 1)
            second = pltpu.roll(part[1], 64 * (1 - cols[1] % 2), 1)
            columns_ref[p, :, x * 256 : x * 256 + 128] = jnp.where(low, first, second).astype(BF16)
            third = pltpu.roll(part[2], 64 * (cols[2] % 2), 1)
            third = jnp.where(low, third, pltpu.roll(third, 64, 1))
            columns_ref[p, :, x * 256 + 128 : x * 256 + 256] = third.astype(BF16)


def early_kernel(group_ref, all_ref, columns_ref, out_ref):
    tags = [tags_of(all_ref, (x,)) for x in range(XN)]
    me = group_ref[0] % XN
    own = by_orbital(spread_lanes(all_ref, (me,)))
    lanes = pl.ds(pl.multiple_of(me * 256, 256), 256)
    fitted = []
    for x in range(XN):
        weights = rows_of(columns_ref, tags[x], lanes)
        rows = jnp.dot(spread_lanes(all_ref, (x,)), weights, preferred_element_type=F32)
        fitted.append(by_orbital(rows.astype(BF16)))
    fitted = jnp.concatenate(fitted, axis=0)
    out_ref[...] = lax.dot_general(own, fitted, NT_DIMS, preferred_element_type=F32)


def late_kernel(far_ref, all_ref, columns_ref, out_ref):
    weights = rows_of(columns_ref, tags_of(far_ref), slice(None))
    rows = jnp.dot(spread_lanes(far_ref), weights, preferred_element_type=F32).astype(BF16)
    for x in range(XN):
        fitted = by_orbital(rows[:, x * 256 : (x + 1) * 256])
        mine = by_orbital(spread_lanes(all_ref, (x,)))
        block = lax.dot_general(mine, fitted, NT_DIMS, preferred_element_type=F32)
        out_ref[x] = jnp.concatenate([block[0:32], block[32:64]], axis=1)


def join_kernel(group_ref, early_ref, late_ref, out_ref):
    high = group_ref[0] >= XN
    late = jnp.concatenate(
        [
            jnp.concatenate([late_ref[x][:, 0:64] for x in range(XN)], axis=1),
            jnp.concatenate([late_ref[x][:, 64:128] for x in range(XN)], axis=1),
        ],
        axis=0,
    )
    early = early_ref[...]
    out_ref[:, 0:256] = jnp.where(high, late, early)
    out_ref[:, 256:512] = jnp.where(high, early, late)


def smem():
    return pl.BlockSpec(memory_space=pltpu.SMEM)


def vmem():
    return pl.BlockSpec(memory_space=pltpu.VMEM)


def in_hbm(value):
    return pltpu.with_memory_space_constraint(value, pltpu.HBM)


def in_vmem(value):
    return pltpu.with_memory_space_constraint(value, pltpu.VMEM)


def staged(parts):
    return pl.pallas_call(
        stage_kernel,
        out_shape=[pltpu.VMEM(p.shape, p.dtype) for p in parts],
        in_specs=[pl.BlockSpec(memory_space=pltpu.HBM)] * len(parts),
        out_specs=[vmem()] * len(parts),
        scratch_shapes=[pltpu.SemaphoreType.DMA] * len(parts),
        compiler_params=pltpu.CompilerParams(vmem_limit_bytes=16 * 2**20),
    )(*[in_hbm(p) for p in parts])


def per_device(occupied, integrals, metric_inv, pattern, support):
    regions = lax.axis_size("blk")
    axes = ("blk", "grp")
    groups = [list(range(XN)), list(range(XN, 2 * XN))]
    region = lax.axis_index("blk").astype(jnp.int32).reshape(1)
    group = lax.axis_index("grp").astype(jnp.int32).reshape(1)

    def spread(value):
        value = jnp.broadcast_to(value[None], (XN,) + value.shape)
        return lax.all_to_all(value, "grp", 0, 0, axis_index_groups=groups)

    pairs = [swap_pairs(j, regions, 8) for j in range(2)]
    asked = []
    for j in range(2):
        asked.append(lax.ppermute(support, axes, pairs[j]))
    (occupied,) = staged([occupied])
    (integrals,) = staged([integrals])
    asked = jnp.concatenate(asked, axis=1)[0]
    wanted = asked[:, None] == jnp.arange(occupied.shape[1], dtype=jnp.int32)[None, :]
    answer = lax.dot_general(wanted.astype(BF16), occupied, NT_DIMS, preferred_element_type=F32)
    answer = answer.astype(BF16)
    answers = []
    for j in range(2):
        answers.append(lax.ppermute(answer[j * OSUP : (j + 1) * OSUP], axes, pairs[j]))
    tag = jnp.pad(pattern[0, 0, :, 2].astype(BF16), (0, occupied.shape[0] - NT))
    answers.append(jnp.broadcast_to(tag, (OSUP, occupied.shape[0])))
    stacked, slots, region = lax.optimization_barrier((jnp.stack(answers, 0), pattern.reshape(-1), region))
    window = spread(stacked)

    message = pl.pallas_call(
        contribution_kernel,
        out_shape=pltpu.VMEM((ROWS, 128), BF16),
        in_specs=[smem(), smem(), vmem(), vmem()],
        out_specs=vmem(),
        scratch_shapes=[pltpu.VMEM((512, 128), F32), pltpu.VMEM((256, 128), F32)],
        name="contribution",
            compiler_params=pltpu.CompilerParams(vmem_limit_bytes=16 * 2**20),
    )(region, slots, in_vmem(window), in_vmem(integrals))

    far = lax.ppermute(message, "grp", [(g, (g + XN) % (2 * XN)) for g in range(2 * XN)])
    everyone = spread(message)
    limit = pltpu.CompilerParams(vmem_limit_bytes=24 * 2**20)
    columns = pl.pallas_call(
        columns_kernel,
        out_shape=pltpu.VMEM((AUXR // AB, AB, XN * 256), BF16),
        in_specs=[vmem(), vmem()],
        out_specs=vmem(),
        compiler_params=limit,
        name="columns",
    )(in_vmem(window), in_hbm(metric_inv.reshape(AUXR // AB, AB, AUXR)))
    early = pl.pallas_call(
        early_kernel,
        out_shape=pltpu.VMEM((BF, XN * BF), F32),
        in_specs=[smem(), vmem(), vmem()],
        out_specs=vmem(),
        compiler_params=limit,
        name="early",
    )(group, in_vmem(everyone), in_vmem(columns))
    late = pl.pallas_call(
        late_kernel,
        out_shape=pltpu.VMEM((XN, BF // 2, 2 * BF), F32),
        in_specs=[vmem(), vmem(), vmem()],
        out_specs=vmem(),
        compiler_params=limit,
        name="late",
    )(in_vmem(far), in_vmem(everyone), in_vmem(columns))
    late = lax.all_to_all(late, "grp", 0, 0, axis_index_groups=groups)
    return pl.pallas_call(
        join_kernel,
        out_shape=jax.ShapeDtypeStruct((BF, 2 * XN * BF), F32),
        in_specs=[smem(), vmem(), vmem()],
        out_specs=vmem(),
        name="join",
            compiler_params=pltpu.CompilerParams(vmem_limit_bytes=16 * 2**20),
    )(group, in_vmem(early), in_vmem(late))


def solution(mesh):
    placed = (
        P("blk", None),
        P("blk", "grp", None, None, None),
        P("blk", None),
        P("blk", "grp", None, None),
        P("blk", None),
    )
    return jax.shard_map(per_device, mesh=mesh, in_specs=placed, out_specs=P(("blk", "grp"), None), check_vma=False)
```
